128 devices in a mesh: gx: 16 (over y, x), gy: 2 (over core), gz: 4 (over z).
Axes of the slice: x: 4, y: 4, z: 4, core: 2. Of those that a mesh axis runs over, the one named last changes fastest.
Arguments:
- density: float32 [384, 128, 512], P('gx', 'gy', 'gz'), may hold values from 0.8 to 1.25
- momentum: float32 [3, 384, 128, 512], P(None, 'gx', 'gy', 'gz'), may hold values from -1.5 to 1.5
- energy: float32 [384, 128, 512], P('gx', 'gy', 'gz'), may hold values from 2 to 3
- increment: float32 [5, 384, 128, 512], P(None, 'gx', 'gy', 'gz'), may hold values from -1.8 to 1.8
Outputs:
- new_state: float32 [5, 384, 128, 512], P(None, 'gx', 'gy', 'gz')
- new_increment: float32 [5, 384, 128, 512], P(None, 'gx', 'gy', 'gz')
The draws below stay inside these ranges and needn't reach their ends.
All inputs are finite; a program needn't handle non-finite values.
Results may differ from the reference program's by a relative error of at most 0.0003.
Values sent between devices are 32-bit elements; how exact they have to be, the bound alone decides.
A program may use at most 128 MiB of HBM per device.

```python
import math
import jax
import jax.numpy as jnp
from jax import lax

NVAR = 5
NX = 384
NY = 128
NZ = 512


def banded_field(key, lower, upper):
    return jax.random.uniform(key, (NX, NY, NZ), jnp.float32, lower, upper)


def draw_density(key, part):
    return banded_field(jax.random.fold_in(key, 11), 0.8, 1.25)


def draw_energy(key, part):
    return banded_field(jax.random.fold_in(key, 23), 2.0, 3.0)


def block_scale(rng, dims, cuts, low, top_value):
    def one(position, shards_of):
        draws = jax.random.uniform(jax.random.fold_in(jax.random.fold_in(rng, 6), position), (shards_of,), jnp.float32, low / len(cuts), top_value / len(cuts))
        return jnp.repeat(jnp.exp(draws), dims[position] // shards_of).reshape((-1,) + (1,) * (len(dims) - position - 1))

    level = one(*cuts[0])
    for cut in cuts[1:]:
        level = level * one(*cut)
    return level


def gaussian(key, shape, width, most, shards=(), kind=jnp.bfloat16):
    gain = block_scale(key, shape, shards, -0.22, 0.18) if shards else 1.0
    result = jax.random.normal(key, shape, jnp.float32) * width * gain
    return jnp.minimum(jnp.maximum(result, -most), most).astype(kind)


def setup_inputs(seed: int = 0) -> dict:
    keys = jax.random.split(jax.random.key(seed), 5)
    return {
        "density": draw_density(jax.random.fold_in(keys[4], 71), 0),
        "momentum": gaussian(keys[1], (3, NX, NY, NZ), 0.3, 1.5, ((1, 16), (2, 2), (3, 4)), jnp.float32),
        "energy": draw_energy(jax.random.fold_in(keys[4], 71), 0),
        "increment": gaussian(keys[3], (NVAR, NX, NY, NZ), 0.3, 1.8, ((1, 16), (2, 2), (3, 4)), jnp.float32),
    }


deriv_alpha = 1.0 / 3.0
filter_alpha = 0.4999
gas_gamma = 1.4
time_step = 0.2
section_a = -5.0 / 9.0
section_b = 15.0 / 16.0

def root_of(coupling):
    return (-1.0 + math.sqrt(1.0 - 4.0 * coupling * coupling)) / (2.0 * coupling)

def signed_power(base_value, exponent):
    magnitude = jnp.power(jnp.float32(abs(base_value)), exponent.astype(jnp.float32))
    if base_value < 0:
        return jnp.where(exponent % 2 == 0, 1.0, -1.0).astype(jnp.float32) * magnitude
    return magnitude

def filter_weights(coupling):
    return [(93.0 + 70.0 * coupling) / 128.0, (7.0 + 18.0 * coupling) / 16.0, (-7.0 + 14.0 * coupling) / 32.0, (1.0 - 2.0 * coupling) / 16.0, (-1.0 + 2.0 * coupling) / 128.0]

def fluxes(cell_block, axis_k):
    density = cell_block[0]
    momentum = cell_block[1:4]
    energy = cell_block[4]
    squared = momentum[0] * momentum[0] + momentum[1] * momentum[1] + momentum[2] * momentum[2]
    pressure = (gas_gamma - 1.0) * (energy - 0.5 * squared / density)
    velocity = momentum[axis_k] / density
    components = [momentum[axis_k], momentum[0] * velocity, momentum[1] * velocity, momentum[2] * velocity, (energy + pressure) * velocity]
    components[axis_k + 1] = components[axis_k + 1] + pressure
    return jnp.stack(components)

def periodic_solve(right_side, coupling):
    decay_rate = root_of(coupling)
    length = right_side.shape[1]
    lines_first = jnp.moveaxis(right_side, 1, 0)

    def advance(previous, element):
        updated = element + decay_rate * previous
        return (updated, updated)
    zero_start = jnp.zeros(lines_first.shape[1:], jnp.float32)
    last_value, forward = lax.scan(advance, zero_start, lines_first)
    closure = 1.0 - decay_rate ** length
    positions = jnp.arange(length, dtype=jnp.int32)
    broadcast_shape = (length,) + (1,) * (lines_first.ndim - 1)
    forward = forward + signed_power(decay_rate, positions + 1).reshape(broadcast_shape) * (last_value / closure)[None]
    first_value, backward = lax.scan(advance, zero_start, forward, reverse=True)
    backward = backward + signed_power(decay_rate, length - positions).reshape(broadcast_shape) * (first_value / closure)[None]
    return jnp.moveaxis(-(decay_rate / coupling) * backward, 0, 1)

def explicit_derivative(field, along_axis):
    summed = jnp.zeros_like(field)
    for offset, weight_n in ((1, 0.75), (2, -0.15), (3, 1.0 / 60.0)):
        summed = summed + weight_n * (jnp.roll(field, -offset, along_axis) - jnp.roll(field, offset, along_axis))
    return summed

def reference(density, momentum, energy, increment):
    fluid_state = jnp.concatenate([density[None], momentum, energy[None]], axis=0)
    flux_x = fluxes(fluid_state, 0)
    compact_side = 7.0 / 9.0 * (jnp.roll(flux_x, -1, 1) - jnp.roll(flux_x, 1, 1)) + 1.0 / 36.0 * (jnp.roll(flux_x, -2, 1) - jnp.roll(flux_x, 2, 1))
    spatial = periodic_solve(compact_side, deriv_alpha)
    spatial = spatial + explicit_derivative(fluxes(fluid_state, 1), 2)
    spatial = spatial + explicit_derivative(fluxes(fluid_state, 2), 3)
    new_increment = section_a * increment - time_step * spatial
    provisional = fluid_state + section_b * new_increment
    weights = filter_weights(filter_alpha)
    filter_side = weights[0] * provisional
    for offset in range(1, 5):
        filter_side = filter_side + weights[offset] / 2.0 * (jnp.roll(provisional, -offset, 1) + jnp.roll(provisional, offset, 1))
    new_state = periodic_solve(filter_side, filter_alpha)
    return (new_state, new_increment)
```

```python
import functools
import math

import jax
import jax.numpy as jnp
from jax import lax
from jax.experimental import pallas as pl
from jax.experimental.pallas import tpu as pltpu
from jax.sharding import PartitionSpec as P

deriv_alpha = 1.0 / 3.0
filter_alpha = 0.4999
gas_gamma = 1.4
time_step = 0.2
section_a = -5.0 / 9.0
section_b = 15.0 / 16.0
MESH = pl.DeviceIdType.MESH
ROWS = 8
FLUX_STEP = 4
NEAR_STEP = 4
UPDATE_STEP = 4
FILTER_STEP = 4
LAST_STEP = 2
VLIM = 56
OUT = pltpu.VMEM
LANES = 128


def root_of(coupling):
    return (-1.0 + math.sqrt(1.0 - 4.0 * coupling * coupling)) / (2.0 * coupling)


deriv_root = root_of(deriv_alpha)
deriv_gain = (
    (25.0 / 36.0)
    / math.sqrt(1.0 - 4.0 * deriv_alpha * deriv_alpha)
    * (1.0 / deriv_root - deriv_root)
)
filter_root = root_of(filter_alpha)


def filter_parts(b):
    w = [
        (93.0 + 70.0 * b) / 128.0,
        (7.0 + 18.0 * b) / 16.0,
        (-7.0 + 14.0 * b) / 32.0,
        (1.0 - 2.0 * b) / 16.0,
        (-1.0 + 2.0 * b) / 128.0,
    ]
    c4 = 8 * w[4]
    c3 = 4 * w[3]
    c2 = 2 * w[2] - 8 * w[4]
    c1 = w[1] - 3 * w[3]
    c0 = w[0] - w[2] + w[4]
    q3 = c4 / (2 * b)
    q2 = (c3 - q3) / (2 * b)
    q1 = (c2 - q2) / (2 * b)
    q0 = (c1 - q1) / (2 * b)
    gain = (c0 - q0) / math.sqrt(1.0 - 4.0 * b * b)
    centre = q0 + q2 / 2 + gain
    return centre, (q1 / 2 + 3 * q3 / 8, q2 / 4, q3 / 8), gain


filter_centre, filter_side, filter_gain = filter_parts(filter_alpha)


def kernel(
    n, zn, rho_h, mom_h, en_h, inc_h,
    Z, S, K2,
    U, FX, FY, FZ, PV, B,
    LP, RP, LR, RR,
    E1, G1, C1, K1, E2, G2, C2,
    in_sem, inc_sem, halo_s, halo_r, self_sem,
    s1, r1, s2, r2, s3, r3, s4, r4,
):
    X = U.shape[1]
    Y = U.shape[2]
    G = Y // ROWS
    V = 5
    per = E1.shape[0] // n
    me = lax.axis_index("gx")
    mey = lax.axis_index("gy")
    mez = lax.axis_index("gz")
    right = lax.rem(me + 1, n)
    left = lax.rem(me + n - 1, n)
    other = 1 - mey
    zup = lax.rem(mez + 1, zn)
    zdown = lax.rem(mez + zn - 1, zn)

    def rows_of(yg):
        return pl.ds(pl.multiple_of(yg * ROWS, ROWS), ROWS)

    def group_at(i):
        return lax.rem(i + G - 1, G)

    def loads(i):
        rows = rows_of(group_at(i))
        return (
            pltpu.make_async_copy(rho_h.at[:, rows, :], U.at[0, :, rows, :], in_sem.at[0, i]),
            pltpu.make_async_copy(mom_h.at[:, :, rows, :], U.at[pl.ds(1, 3), :, rows, :], in_sem.at[1, i]),
            pltpu.make_async_copy(en_h.at[:, rows, :], U.at[4, :, rows, :], in_sem.at[2, i]),
        )

    for i in range(G):
        for c in loads(i):
            c.start()
    inc_load = pltpu.make_async_copy(inc_h, S, inc_sem)
    inc_load.start()

    barrier = pltpu.get_barrier_semaphore()

    def greet(k, _):
        pl.semaphore_signal(
            barrier, inc=1, device_id={"gx": lax.rem(me + k, n)}, device_id_type=MESH
        )
        return 0

    lax.fori_loop(1, n, greet, 0)
    pl.semaphore_signal(barrier, inc=1, device_id={"gy": other}, device_id_type=MESH)
    pl.semaphore_signal(barrier, inc=1, device_id={"gz": zup}, device_id_type=MESH)
    pl.semaphore_signal(barrier, inc=1, device_id={"gz": zdown}, device_id_type=MESH)

    lane = lax.broadcasted_iota(jnp.int32, (ROWS, LANES), 1)
    zero = jnp.zeros((ROWS, LANES), jnp.float32)
    zeros = (zero,) * V

    apart = lax.rem(
        lax.broadcasted_iota(jnp.int32, (2 * LANES, LANES), 0)
        + (2 * LANES - lax.broadcasted_iota(jnp.int32, (2 * LANES, LANES), 1)),
        LANES,
    )
    band = jnp.zeros((2 * LANES, LANES), jnp.float32)
    for o, weight in ((1, 45.0), (2, -9.0), (3, 1.0)):
        band = jnp.where(apart == o, weight, band)
        band = jnp.where(apart == LANES - o, -weight, band)
    B[...] = band.astype(jnp.bfloat16)

    def flux_rows(i, _):
        for c in loads(i):
            c.wait()
        yg = group_at(i)
        rows = rows_of(yg)
        rows_y = pl.ds(pl.multiple_of(yg * ROWS + ROWS, ROWS), ROWS)

        def flux_cells(j, carry):
            ef, g, lp, rp, weight = carry
            ef, g, lp, rp = list(ef), list(g), list(lp), list(rp)
            for u in range(FLUX_STEP):
                x = X - 1 - u - j * FLUX_STEP
                rho = U[0, x, rows, :]
                m0 = U[1, x, rows, :]
                m1 = U[2, x, rows, :]
                m2 = U[3, x, rows, :]
                en = U[4, x, rows, :]
                inv = 1.0 / rho
                v0 = m0 * inv
                v1 = m1 * inv
                v2 = m2 * inv
                a00 = m0 * v0
                a11 = m1 * v1
                a22 = m2 * v2
                a01 = m0 * v1
                a02 = m0 * v2
                a12 = m1 * v2
                pressure = (gas_gamma - 1.0) * (en - 0.5 * (a00 + a11 + a22))
                total = en + pressure
                fx = (m0, a00 + pressure, a01, a02, total * v0)
                fy = (m1, a01, a11 + pressure, a12, total * v1)
                fz = (m2, a02, a12, a22 + pressure, total * v2)
                keep_l = lane < 3 * x + 3
                keep_r = lane < 3 * x + 6
                for v in range(V):
                    FX[v, x + 1, rows, :] = fx[v]
                    FY[v, x, rows_y, :] = fy[v]
                    FZ[v, x, rows, :] = fz[v]
                    Z[v, x, rows, :] = g[v]
                    g[v] = deriv_root * (g[v] + fx[v])
                    ef[v] = ef[v] + weight * fx[v]
                    turned = pltpu.roll(fz[v], 3 * x + 3, 1)
                    lp[v] = jnp.where(keep_l, turned, lp[v])
                    rp[v] = jnp.where(keep_r, turned, rp[v])
                weight = weight * deriv_root
            return tuple(ef), tuple(g), tuple(lp), tuple(rp), weight

        ef, g, lp, rp, _ = lax.fori_loop(
            0, X // FLUX_STEP, flux_cells,
            (zeros, zeros, zeros, zeros, jnp.float32(deriv_root)),
        )
        for v in range(V):
            E1[v * G + yg] = ef[v]
            E1[V * G + v * G + yg] = g[v]
            LP[v, rows, :] = lp[v]
            RP[v, rows, :] = rp[v]
        return 0

    def slot_of(owner, block):
        return jnp.where(owner < n // 2, block, n - 1 - block)

    def chunk(i):
        return pl.ds(i * per, per)

    def ends_copy(E, gathered, ssem, rsem, k):
        owner = lax.rem(me + k, n)
        return pltpu.make_async_remote_copy(
            src_ref=E.at[chunk(owner)],
            dst_ref=gathered.at[chunk(slot_of(owner, me))],
            send_sem=ssem.at[k],
            recv_sem=rsem.at[k],
            device_id={"gx": owner},
            device_id_type=MESH,
        )

    def send_ends(E, gathered, ssem, rsem):
        def one(k, _):
            ends_copy(E, gathered, ssem, rsem, k).start()
            return 0

        lax.fori_loop(1, n, one, 0)
        own = pltpu.make_async_copy(
            E.at[chunk(me)], gathered.at[chunk(slot_of(me, me))], self_sem
        )
        own.start()
        own.wait()

    def carry_copy(C, K, ssem, rsem, k):
        block = lax.rem(me + k, n)
        return pltpu.make_async_remote_copy(
            src_ref=C.at[chunk(slot_of(me, block))],
            dst_ref=K.at[chunk(me)],
            send_sem=ssem.at[k],
            recv_sem=rsem.at[k],
            device_id={"gx": block},
            device_id_type=MESH,
        )

    def wait_all(make):
        def one(k, _):
            make(k).wait()
            return 0

        lax.fori_loop(1, n, one, 0)

    def carries(gathered, C, K, root, ssem, rsem):
        block_root = root**X
        scale = 1.0 / (1.0 - block_root**n)

        def total(s, h):
            return tuple(gathered[s * per + q] + block_root * h[q] for q in range(per))

        h = lax.fori_loop(0, n, total, (zero,) * per)

        def step(s, c):
            for q in range(per):
                C[s * per + q] = c[q]
            return tuple(gathered[s * per + q] + block_root * c[q] for q in range(per))

        lax.fori_loop(0, n, step, tuple(h[q] * scale for q in range(per)))

        def one(k, _):
            carry_copy(C, K, ssem, rsem, k).start()
            return 0

        lax.fori_loop(1, n, one, 0)
        own = pltpu.make_async_copy(
            C.at[chunk(slot_of(me, me))], K.at[chunk(me)], self_sem
        )
        own.start()
        own.wait()

    def remote(src, dst, i, device):
        return pltpu.make_async_remote_copy(
            src_ref=src, dst_ref=dst, send_sem=halo_s.at[i], recv_sem=halo_r.at[i],
            device_id=device, device_id_type=MESH,
        )

    halo = [
        remote(LP, LR, 0, {"gz": zup}),
        remote(RP, RR, 1, {"gz": zdown}),
        remote(FY.at[:, :, pl.ds(Y, ROWS), :], FY.at[:, :, pl.ds(0, ROWS), :], 2, {"gy": other}),
        remote(FY.at[:, :, pl.ds(ROWS, ROWS), :], FY.at[:, :, pl.ds(Y + ROWS, ROWS), :], 3, {"gy": other}),
        remote(FX.at[:, pl.ds(X, 1)], FX.at[:, pl.ds(0, 1)], 4, {"gx": right}),
        remote(FX.at[:, pl.ds(1, 1)], FX.at[:, pl.ds(X + 1, 1)], 5, {"gx": left}),
    ]
    lax.fori_loop(0, 2, flux_rows, 0)
    pl.semaphore_wait(barrier, n + 2)
    halo[2].start()
    halo[3].start()
    lax.fori_loop(2, G, flux_rows, 0)
    send_ends(E1, G1, s1, r1)
    for i in (0, 1, 4, 5):
        halo[i].start()

    inc_load.wait()
    halo[2].wait()
    halo[3].wait()
    k1, k2, k3 = (-time_step * w for w in (0.75, -0.15, 1.0 / 60.0))

    z_scale = -time_step / 60.0

    def yz_plane(x, _):
        hz = FZ[:, x].reshape(V * Y, LANES)
        head = hz.astype(jnp.bfloat16)
        rest = hz - head.astype(jnp.float32)
        middle = rest.astype(jnp.bfloat16)
        tail = (rest - middle.astype(jnp.float32)).astype(jnp.bfloat16)
        dz = jnp.dot(
            jnp.concatenate([head, middle], axis=1), B[...], preferred_element_type=jnp.float32
        ) + jnp.dot(tail, B[0:LANES, :], preferred_element_type=jnp.float32)
        for v in range(V):
            for yg in range(G):
                base = ROWS + yg * ROWS
                out = slice(yg * ROWS, yg * ROWS + ROWS)
                at = v * Y + yg * ROWS

                def both(o):
                    return (
                        FY[v, x, base + o : base + o + ROWS, :]
                        - FY[v, x, base - o : base - o + ROWS, :]
                    )

                S[v, x, out, :] = (
                    (section_a * S[v, x, out, :] + z_scale * dz[at : at + ROWS, :])
                    + (k1 * both(1) + k2 * both(2) + k3 * both(3))
                )
        return 0

    lax.fori_loop(0, X, yz_plane, 0)

    wait_all(lambda k: ends_copy(E1, G1, s1, r1, k))
    carries(G1, C1, K1, deriv_root, s2, r2)

    halo[0].wait()
    halo[1].wait()
    third = lax.rem(lane, 3)
    weights = (k1, k2, k3)

    def z_edges(v, _):
        for yg in range(G):
            rows = slice(yg * ROWS, yg * ROWS + ROWS)
            dl = LR[v, rows, :] - LP[v, rows, :]
            dr = RR[v, rows, :] - RP[v, rows, :]
            low = zero
            high = zero
            for o in (1, 2, 3):
                low = low - jnp.where(third < o, weights[o - 1] * pltpu.roll(dl, o, 1), 0.0)
                high = high + jnp.where(
                    third >= 3 - o, weights[o - 1] * pltpu.roll(dr, LANES - o, 1), 0.0
                )
            LR[v, rows, :] = low
            RR[v, rows, :] = high
        return 0

    lax.fori_loop(0, V, z_edges, 0)

    halo[4].wait()
    halo[5].wait()
    near = -time_step / 12.0
    far = -time_step * deriv_gain

    def near_rows(yg, _):
        rows = rows_of(yg)
        low = [LR[v, rows, :] for v in range(V)]
        high = [RR[v, rows, :] for v in range(V)]
        rim = (lane < 3) | (lane >= LANES - 3)

        def near_cells(j, f):
            f = list(f)
            x0 = j * NEAR_STEP
            for v in range(V):
                window = [FX[v, x0 + u, rows, :] for u in range(NEAR_STEP + 2)]
                for u in range(NEAR_STEP):
                    x = x0 + u
                    edge = jnp.where(lane < 3 * x + 3, high[v], low[v])
                    edge = jnp.where(rim, pltpu.roll(edge, 125 - 3 * x, 1), 0.0)
                    S[v, x, rows, :] = (
                        (S[v, x, rows, :] + edge)
                        + near * (window[u + 2] - window[u])
                        + far * (Z[v, x, rows, :] - f[v])
                    )
                    f[v] = deriv_root * (f[v] + window[u + 1])
            return tuple(f)

        lax.fori_loop(0, X // NEAR_STEP, near_cells, zeros)
        return 0

    lax.fori_loop(0, G, near_rows, 0)

    wait_all(lambda k: carry_copy(C1, K1, s2, r2, k))

    def update_rows(yg, _):
        rows = rows_of(yg)
        cf = [(-far * deriv_root ** (X - 1)) * K1[v * G + yg] for v in range(V)]
        cb = [far * K1[V * G + v * G + yg] for v in range(V)]

        def update_cells(j, carry):
            ef, g, wf, wb, weight = carry
            ef, g = list(ef), list(g)
            for u in range(UPDATE_STEP):
                x = X - 1 - u - j * UPDATE_STEP
                for v in range(V):
                    s = S[v, x, rows, :] + (wf * cf[v] + wb * cb[v])
                    p = U[v, x, rows, :] + section_b * s
                    S[v, x, rows, :] = s
                    PV[v, x + 3, rows, :] = p
                    Z[v, x, rows, :] = g[v]
                    g[v] = filter_root * (g[v] + p)
                    ef[v] = ef[v] + weight * p
                wf = wf * (1.0 / deriv_root)
                wb = wb * deriv_root
                weight = weight * filter_root
            return tuple(ef), tuple(g), wf, wb, weight

        ef, g, _, _, _ = lax.fori_loop(
            0, X // UPDATE_STEP, update_cells,
            (zeros, zeros, jnp.float32(1.0), jnp.float32(1.0), jnp.float32(filter_root)),
        )
        for v in range(V):
            E2[v * G + yg] = ef[v]
            E2[V * G + v * G + yg] = g[v]
        return 0

    lax.fori_loop(0, G, update_rows, 0)

    send_ends(E2, G2, s3, r3)
    sides = [
        remote(PV.at[:, pl.ds(X, 3)], PV.at[:, pl.ds(0, 3)], 6, {"gx": right}),
        remote(PV.at[:, pl.ds(3, 3)], PV.at[:, pl.ds(X + 3, 3)], 7, {"gx": left}),
    ]
    for c in sides:
        c.start()

    wait_all(lambda k: ends_copy(E2, G2, s3, r3, k))
    carries(G2, C2, K2, filter_root, s4, r4)

    sides[0].wait()
    sides[1].wait()
    t1, t2, t3 = filter_side

    def filter_rows(yg, _):
        rows = rows_of(yg)

        def filter_cells(j, f):
            f = list(f)
            x0 = j * FILTER_STEP
            for v in range(V):
                w = [PV[v, x0 + u, rows, :] for u in range(FILTER_STEP + 6)]
                for u in range(FILTER_STEP):
                    x = x0 + u
                    Z[v, x, rows, :] = (
                        filter_centre * w[u + 3]
                        + filter_gain * (Z[v, x, rows, :] + f[v])
                        + t1 * (w[u + 4] + w[u + 2])
                        + t2 * (w[u + 5] + w[u + 1])
                        + t3 * (w[u + 6] + w[u])
                    )
                    f[v] = filter_root * (f[v] + w[u + 3])
            return tuple(f)

        lax.fori_loop(0, X // FILTER_STEP, filter_cells, zeros)
        return 0

    lax.fori_loop(0, G, filter_rows, 0)
    wait_all(lambda k: carry_copy(C2, K2, s4, r4, k))


def last_kernel(z_ref, s_ref, carry_ref, state_h, inc_h, out, sem):
    X = z_ref.shape[1]
    G = z_ref.shape[2] // ROWS
    inc_out = pltpu.make_async_copy(s_ref, inc_h, sem.at[X // LAST_STEP])
    parts = X // LAST_STEP

    def state_out(j):
        planes = pl.ds(j * LAST_STEP, LAST_STEP)
        return pltpu.make_async_copy(out.at[:, planes], state_h.at[:, planes], sem.at[j])

    inc_out.start()
    for j in range(parts):
        for v in range(5):
            for yg in range(G):
                rows = slice(yg * ROWS, yg * ROWS + ROWS)
                ahead = carry_ref[v * G + yg]
                behind = carry_ref[(5 + v) * G + yg]
                for u in range(LAST_STEP):
                    x = j * LAST_STEP + u
                    out[v, x, rows, :] = z_ref[v, x, rows, :] + (
                        (filter_gain * filter_root**x) * ahead
                        + (filter_gain * filter_root ** (X - 1 - x)) * behind
                    )
        state_out(j).start()
    for j in range(parts):
        state_out(j).wait()
    inc_out.wait()


def section(n, zn, density, momentum, energy, increment):
    X, Y, L = density.shape
    G = Y // ROWS
    ends = 2 * 5 * G
    f32 = jnp.float32
    pack = pltpu.VMEM((5, Y, L), f32)
    end = pltpu.VMEM((ends, ROWS, L), f32)
    many = pltpu.SemaphoreType.DMA((n,))
    anywhere = pl.BlockSpec(memory_space=pl.ANY)
    hbm = pl.BlockSpec(memory_space=pltpu.HBM)
    vmem = pl.BlockSpec(memory_space=pltpu.VMEM)
    part, register, carry = pl.pallas_call(
        functools.partial(kernel, n, zn),
        out_shape=(
            OUT((5, X, Y, L), f32),
            OUT((5, X, Y, L), f32),
            OUT((ends, ROWS, L), f32),
        ),
        in_specs=[hbm] * 4,
        out_specs=(vmem,) * 3,
        scratch_shapes=[
            pltpu.VMEM((5, X, Y, L), f32),
            pltpu.VMEM((5, X + 2, Y, L), f32),
            pltpu.VMEM((5, X, Y + 2 * ROWS, L), f32),
            pltpu.VMEM((5, X, Y, L), f32),
            pltpu.VMEM((5, X + 6, Y, L), f32),
            pltpu.VMEM((2 * L, L), jnp.bfloat16),
            pack, pack, pack, pack,
            end, end, end, end, end, end, end,
            pltpu.SemaphoreType.DMA((3, G)),
            pltpu.SemaphoreType.DMA,
            pltpu.SemaphoreType.DMA((8,)),
            pltpu.SemaphoreType.DMA((8,)),
            pltpu.SemaphoreType.DMA,
            many, many, many, many, many, many, many, many,
        ],
        compiler_params=pltpu.CompilerParams(
            collective_id=0, has_side_effects=True, vmem_limit_bytes=VLIM * 1024 * 1024
        ),
    )(density, momentum, energy, increment)
    return pl.pallas_call(
        last_kernel,
        out_shape=(
            jax.ShapeDtypeStruct((5, X, Y, L), f32),
            jax.ShapeDtypeStruct((5, X, Y, L), f32),
        ),
        in_specs=[vmem] * 3,
        out_specs=(hbm, hbm),
        scratch_shapes=[
            pltpu.VMEM((5, X, Y, L), f32),
            pltpu.SemaphoreType.DMA((X // LAST_STEP + 1,)),
        ],
        compiler_params=pltpu.CompilerParams(vmem_limit_bytes=16 * 1024 * 1024),
    )(part, register, carry)


def solution(mesh):
    in_specs = (
        P("gx", "gy", "gz"),
        P(None, "gx", "gy", "gz"),
        P("gx", "gy", "gz"),
        P(None, "gx", "gy", "gz"),
    )
    out_specs = (P(None, "gx", "gy", "gz"), P(None, "gx", "gy", "gz"))
    return jax.shard_map(
        functools.partial(section, mesh.shape["gx"], mesh.shape["gz"]),
        mesh=mesh,
        in_specs=in_specs,
        out_specs=out_specs,
        check_vma=False,
    )
```

```python
import functools
import math

import jax
import jax.numpy as jnp
from jax import lax
from jax.experimental import pallas as pl
from jax.experimental.pallas import tpu as pltpu
from jax.sharding import PartitionSpec as P

deriv_alpha = 1.0 / 3.0
filter_alpha = 0.4999
gas_gamma = 1.4
time_step = 0.2
section_a = -5.0 / 9.0
section_b = 15.0 / 16.0
MESH = pl.DeviceIdType.MESH
ROWS = 8
FLUX_STEP = 4
NEAR_STEP = 3
UPDATE_STEP = 4
FILTER_STEP = 3
LAST_STEP = 2
VLIM = 56
OUT = pltpu.VMEM
LANES = 128


def root_of(coupling):
    return (-1.0 + math.sqrt(1.0 - 4.0 * coupling * coupling)) / (2.0 * coupling)


deriv_root = root_of(deriv_alpha)
deriv_gain = (
    (25.0 / 36.0)
    / math.sqrt(1.0 - 4.0 * deriv_alpha * deriv_alpha)
    * (1.0 / deriv_root - deriv_root)
)
filter_root = root_of(filter_alpha)


def filter_parts(b):
    w = [
        (93.0 + 70.0 * b) / 128.0,
        (7.0 + 18.0 * b) / 16.0,
        (-7.0 + 14.0 * b) / 32.0,
        (1.0 - 2.0 * b) / 16.0,
        (-1.0 + 2.0 * b) / 128.0,
    ]
    c4 = 8 * w[4]
    c3 = 4 * w[3]
    c2 = 2 * w[2] - 8 * w[4]
    c1 = w[1] - 3 * w[3]
    c0 = w[0] - w[2] + w[4]
    q3 = c4 / (2 * b)
    q2 = (c3 - q3) / (2 * b)
    q1 = (c2 - q2) / (2 * b)
    q0 = (c1 - q1) / (2 * b)
    gain = (c0 - q0) / math.sqrt(1.0 - 4.0 * b * b)
    centre = q0 + q2 / 2 + gain
    return centre, (q1 / 2 + 3 * q3 / 8, q2 / 4, q3 / 8), gain


filter_centre, filter_side, filter_gain = filter_parts(filter_alpha)


def kernel(
    n, zn, rho_h, mom_h, en_h, inc_h,
    Z, S, K2,
    U, FX, FY, FZ, PV, B,
    LP, RP, LR, RR,
    E1, G1, C1, K1, E2, G2, C2,
    PE, FT, CN, DN,
    in_sem, inc_sem, halo_s, halo_r,
    s1, r1, s2, r2, s3, r3, s4, r4,
):
    X = U.shape[1]
    Y = U.shape[2]
    G = Y // ROWS
    V = 5
    T = X - 3
    per = E1.shape[0] // n
    order = sorted(range(1, n), key=lambda k: (-min(k % 4, 4 - k % 4) - min(k // 4, 4 - k // 4), k))
    me = lax.axis_index("gx")
    mey = lax.axis_index("gy")
    mez = lax.axis_index("gz")
    right = lax.rem(me + 1, n)
    left = lax.rem(me + n - 1, n)
    other = 1 - mey
    zup = lax.rem(mez + 1, zn)
    zdown = lax.rem(mez + zn - 1, zn)

    def rows_of(yg):
        return pl.ds(pl.multiple_of(yg * ROWS, ROWS), ROWS)

    def group_at(i):
        return lax.rem(i + G - 1, G)

    def loads(i):
        rows = rows_of(group_at(i))
        return (
            pltpu.make_async_copy(rho_h.at[:, rows, :], U.at[0, :, rows, :], in_sem.at[0, i]),
            pltpu.make_async_copy(mom_h.at[:, :, rows, :], U.at[pl.ds(1, 3), :, rows, :], in_sem.at[1, i]),
            pltpu.make_async_copy(en_h.at[:, rows, :], U.at[4, :, rows, :], in_sem.at[2, i]),
        )

    for i in range(G):
        for c in loads(i):
            c.start()
    inc_load = pltpu.make_async_copy(inc_h, S, inc_sem)
    inc_load.start()

    barrier = pltpu.get_barrier_semaphore()

    def greet(k, _):
        pl.semaphore_signal(
            barrier, inc=1, device_id={"gx": lax.rem(me + k, n)}, device_id_type=MESH
        )
        return 0

    lax.fori_loop(1, n, greet, 0)
    pl.semaphore_signal(barrier, inc=1, device_id={"gy": other}, device_id_type=MESH)
    pl.semaphore_signal(barrier, inc=1, device_id={"gz": zup}, device_id_type=MESH)
    pl.semaphore_signal(barrier, inc=1, device_id={"gz": zdown}, device_id_type=MESH)

    lane = lax.broadcasted_iota(jnp.int32, (ROWS, LANES), 1)
    zero = jnp.zeros((ROWS, LANES), jnp.float32)
    zeros = (zero,) * V

    apart = lax.rem(
        lax.broadcasted_iota(jnp.int32, (2 * LANES, LANES), 0)
        + (2 * LANES - lax.broadcasted_iota(jnp.int32, (2 * LANES, LANES), 1)),
        LANES,
    )
    band = jnp.zeros((2 * LANES, LANES), jnp.float32)
    for o, weight in ((1, 45.0), (2, -9.0), (3, 1.0)):
        band = jnp.where(apart == o, weight, band)
        band = jnp.where(apart == LANES - o, -weight, band)
    B[...] = band.astype(jnp.bfloat16)

    def flux_rows(i, _):
        for c in loads(i):
            c.wait()
        yg = group_at(i)
        rows = rows_of(yg)
        rows_y = pl.ds(pl.multiple_of(yg * ROWS + ROWS, ROWS), ROWS)

        def flux_cells(j, carry):
            ef, g, lp, rp, weight = carry
            ef, g, lp, rp = list(ef), list(g), list(lp), list(rp)
            for u in range(FLUX_STEP):
                x = X - 1 - u - j * FLUX_STEP
                rho = U[0, x, rows, :]
                m0 = U[1, x, rows, :]
                m1 = U[2, x, rows, :]
                m2 = U[3, x, rows, :]
                en = U[4, x, rows, :]
                inv = 1.0 / rho
                v0 = m0 * inv
                v1 = m1 * inv
                v2 = m2 * inv
                a00 = m0 * v0
                a11 = m1 * v1
                a22 = m2 * v2
                a01 = m0 * v1
                a02 = m0 * v2
                a12 = m1 * v2
                pressure = (gas_gamma - 1.0) * (en - 0.5 * (a00 + a11 + a22))
                total = en + pressure
                fx = (m0, a00 + pressure, a01, a02, total * v0)
                fy = (m1, a01, a11 + pressure, a12, total * v1)
                fz = (m2, a02, a12, a22 + pressure, total * v2)
                now = jnp.where(x < T, weight, 0.0)
                keep_l = lane < 3 * x + 3
                keep_r = lane < 3 * x + 6
                for v in range(V):
                    FX[v, x + 1, rows, :] = fx[v]
                    FY[v, x, rows_y, :] = fy[v]
                    FZ[v, x, rows, :] = fz[v]
                    Z[v, x, rows, :] = g[v]
                    g[v] = deriv_root * (g[v] + fx[v])
                    ef[v] = ef[v] + now * fx[v]
                    turned = pltpu.roll(fz[v], 3 * x + 3, 1)
                    lp[v] = jnp.where(keep_l, turned, lp[v])
                    rp[v] = jnp.where(keep_r, turned, rp[v])
                weight = jnp.where(x < T, weight * deriv_root, weight)
            return tuple(ef), tuple(g), tuple(lp), tuple(rp), weight

        ef, g, lp, rp, _ = lax.fori_loop(
            0, X // FLUX_STEP, flux_cells,
            (zeros, zeros, zeros, zeros, jnp.float32(deriv_root)),
        )
        for v in range(V):
            FT[v * G + yg] = ef[v]
            f = ef[v]
            for x in range(T, X):
                f = deriv_root * (f + FX[v, x + 1, rows, :])
            E1[v * G + yg] = f
            E1[V * G + v * G + yg] = g[v]
            LP[v, rows, :] = lp[v]
            RP[v, rows, :] = rp[v]
        return 0

    def slot_of(owner, block):
        return jnp.where(owner < n // 2, block, n - 1 - block)

    def chunk(i):
        return pl.ds(i * per, per)

    def ends_copy(E, gathered, ssem, rsem, k):
        owner = lax.rem(me + k, n)
        return pltpu.make_async_remote_copy(
            src_ref=E.at[chunk(owner)],
            dst_ref=gathered.at[chunk(slot_of(owner, me))],
            send_sem=ssem.at[k],
            recv_sem=rsem.at[k],
            device_id={"gx": owner},
            device_id_type=MESH,
        )

    def keep_own(src, dst, start, end):
        for q in range(per):
            dst[end * per + q] = src[start * per + q]

    def send_ends(E, gathered, ssem, rsem):
        for k in order:
            ends_copy(E, gathered, ssem, rsem, k).start()
        keep_own(E, gathered, me, slot_of(me, me))

    def carry_copy(C, K, ssem, rsem, k):
        block = lax.rem(me + k, n)
        return pltpu.make_async_remote_copy(
            src_ref=C.at[chunk(slot_of(me, block))],
            dst_ref=K.at[chunk(me)],
            send_sem=ssem.at[k],
            recv_sem=rsem.at[k],
            device_id={"gx": block},
            device_id_type=MESH,
        )

    def wait_all(make):
        def one(k, _):
            make(k).wait()
            return 0

        lax.fori_loop(1, n, one, 0)

    def carries(gathered, C, K, root, ssem, rsem):
        block_root = root**X
        scale = 1.0 / (1.0 - block_root**n)

        def total(s, h):
            return tuple(gathered[s * per + q] + block_root * h[q] for q in range(per))

        h = lax.fori_loop(0, n, total, (zero,) * per)

        def step(s, c):
            for q in range(per):
                C[s * per + q] = c[q]
            return tuple(gathered[s * per + q] + block_root * c[q] for q in range(per))

        lax.fori_loop(0, n, step, tuple(h[q] * scale for q in range(per)))

        for k in order:
            carry_copy(C, K, ssem, rsem, k).start()
        keep_own(C, K, slot_of(me, me), me)

    def remote(src, dst, i, device):
        return pltpu.make_async_remote_copy(
            src_ref=src, dst_ref=dst, send_sem=halo_s.at[i], recv_sem=halo_r.at[i],
            device_id=device, device_id_type=MESH,
        )

    halo = [
        remote(LP, LR, 0, {"gz": zup}),
        remote(RP, RR, 1, {"gz": zdown}),
        remote(FY.at[:, :, pl.ds(Y, ROWS), :], FY.at[:, :, pl.ds(0, ROWS), :], 2, {"gy": other}),
        remote(FY.at[:, :, pl.ds(ROWS, ROWS), :], FY.at[:, :, pl.ds(Y + ROWS, ROWS), :], 3, {"gy": other}),
        remote(FX.at[:, pl.ds(X, 1)], FX.at[:, pl.ds(0, 1)], 4, {"gx": right}),
        remote(FX.at[:, pl.ds(1, 1)], FX.at[:, pl.ds(X + 1, 1)], 5, {"gx": left}),
    ]
    lax.fori_loop(0, G, flux_rows, 0)
    pl.semaphore_wait(barrier, n + 2)
    send_ends(E1, G1, s1, r1)
    halo[2].start()
    halo[3].start()
    for i in (0, 1, 4, 5):
        halo[i].start()

    inc_load.wait()
    halo[2].wait()
    halo[3].wait()
    k1, k2, k3 = (-time_step * w for w in (0.75, -0.15, 1.0 / 60.0))

    z_scale = -time_step / 60.0

    def yz_plane(x, _):
        hz = FZ[:, x].reshape(V * Y, LANES)
        head = hz.astype(jnp.bfloat16)
        rest = hz - head.astype(jnp.float32)
        middle = rest.astype(jnp.bfloat16)
        tail = (rest - middle.astype(jnp.float32)).astype(jnp.bfloat16)
        dz = jnp.dot(
            jnp.concatenate([head, middle], axis=1), B[...], preferred_element_type=jnp.float32
        ) + jnp.dot(tail, B[0:LANES, :], preferred_element_type=jnp.float32)
        for v in range(V):
            for yg in range(G):
                base = ROWS + yg * ROWS
                out = slice(yg * ROWS, yg * ROWS + ROWS)
                at = v * Y + yg * ROWS

                def both(o):
                    return (
                        FY[v, x, base + o : base + o + ROWS, :]
                        - FY[v, x, base - o : base - o + ROWS, :]
                    )

                S[v, x, out, :] = (
                    (section_a * S[v, x, out, :] + z_scale * dz[at : at + ROWS, :])
                    + (k1 * both(1) + k2 * both(2) + k3 * both(3))
                )
        return 0

    lax.fori_loop(0, 16, yz_plane, 0)

    wait_all(lambda k: ends_copy(E1, G1, s1, r1, k))
    carries(G1, C1, K1, deriv_root, s2, r2)
    lax.fori_loop(16, X, yz_plane, 0)

    halo[0].wait()
    halo[1].wait()
    third = lax.rem(lane, 3)
    weights = (k1, k2, k3)

    def z_edges(v, _):
        for yg in range(G):
            rows = slice(yg * ROWS, yg * ROWS + ROWS)
            dl = LR[v, rows, :] - LP[v, rows, :]
            dr = RR[v, rows, :] - RP[v, rows, :]
            low = zero
            high = zero
            for o in (1, 2, 3):
                low = low - jnp.where(third < o, weights[o - 1] * pltpu.roll(dl, o, 1), 0.0)
                high = high + jnp.where(
                    third >= 3 - o, weights[o - 1] * pltpu.roll(dr, LANES - o, 1), 0.0
                )
            LR[v, rows, :] = low
            RR[v, rows, :] = high
        return 0

    lax.fori_loop(0, V, z_edges, 0)

    halo[4].wait()
    halo[5].wait()
    near = -time_step / 12.0
    far = -time_step * deriv_gain
    rim = (lane < 3) | (lane >= LANES - 3)

    def near_cells(rows, v, x0, count, f, low, high):
        window = [FX[v, x0 + u, rows, :] for u in range(count + 2)]
        out = []
        for u in range(count):
            x = x0 + u
            edge = jnp.where(lane < 3 * x + 3, high, low)
            edge = jnp.where(rim, pltpu.roll(edge, 125 - 3 * x, 1), 0.0)
            s = (
                (S[v, x, rows, :] + edge)
                + near * (window[u + 2] - window[u])
                + far * (Z[v, x, rows, :] - f)
            )
            S[v, x, rows, :] = s
            out.append(s)
            f = deriv_root * (f + window[u + 1])
        return f, out

    def outer_rows(yg, _):
        rows = rows_of(yg)
        for v in range(V):
            low = LR[v, rows, :]
            high = RR[v, rows, :]
            for side, x0, f in ((0, T, FT[v * G + yg]), (1, 0, zero)):
                _, found = near_cells(rows, v, x0, 3, f, low, high)
                for u in range(3):
                    PE[side, v, u, rows, :] = U[v, x0 + u, rows, :] + section_b * found[u]
        return 0

    lax.fori_loop(0, G, outer_rows, 0)
    sides = [
        remote(PE.at[0], PV.at[:, pl.ds(0, 3)], 6, {"gx": right}),
        remote(PE.at[1], PV.at[:, pl.ds(X + 3, 3)], 7, {"gx": left}),
    ]
    sides[0].start()
    sides[1].start()

    def near_rows(yg, _):
        rows = rows_of(yg)
        low = [LR[v, rows, :] for v in range(V)]
        high = [RR[v, rows, :] for v in range(V)]
        start = []
        for v in range(V):
            f = zero
            for x in range(3):
                f = deriv_root * (f + FX[v, x + 1, rows, :])
            start.append(f)

        def cells(j, f):
            x0 = 3 + j * NEAR_STEP
            return tuple(
                near_cells(rows, v, x0, NEAR_STEP, f[v], low[v], high[v])[0] for v in range(V)
            )

        lax.fori_loop(0, (X - 6) // NEAR_STEP, cells, tuple(start))
        return 0

    lax.fori_loop(0, G, near_rows, 0)

    wait_all(lambda k: carry_copy(C1, K1, s2, r2, k))
    lines = V * G
    beyond = [
        remote(K1.at[pl.ds(0, lines)], CN, 8, {"gx": right}),
        remote(K1.at[pl.ds(lines, lines)], DN, 9, {"gx": left}),
    ]

    def update_rows(yg, _):
        rows = rows_of(yg)
        cf = [(-far * deriv_root ** (X - 1)) * K1[v * G + yg] for v in range(V)]
        cb = [far * K1[V * G + v * G + yg] for v in range(V)]

        def update_cells(j, carry):
            ef, g, wf, wb, weight = carry
            ef, g = list(ef), list(g)
            for u in range(UPDATE_STEP):
                x = X - 1 - u - j * UPDATE_STEP
                for v in range(V):
                    s = S[v, x, rows, :] + (wf * cf[v] + wb * cb[v])
                    p = U[v, x, rows, :] + section_b * s
                    S[v, x, rows, :] = s
                    PV[v, x + 3, rows, :] = p
                    Z[v, x, rows, :] = g[v]
                    g[v] = filter_root * (g[v] + p)
                    ef[v] = ef[v] + weight * p
                wf = wf * (1.0 / deriv_root)
                wb = wb * deriv_root
                weight = weight * filter_root
            return tuple(ef), tuple(g), wf, wb, weight

        ef, g, _, _, _ = lax.fori_loop(
            0, X // UPDATE_STEP, update_cells,
            (zeros, zeros, jnp.float32(1.0), jnp.float32(1.0), jnp.float32(filter_root)),
        )
        for v in range(V):
            E2[v * G + yg] = ef[v]
            E2[V * G + v * G + yg] = g[v]
        return 0

    lax.fori_loop(0, G, update_rows, 0)

    send_ends(E2, G2, s3, r3)
    beyond[0].start()
    beyond[1].start()
    t1, t2, t3 = filter_side

    def filter_rows(yg, _):
        rows = rows_of(yg)
        start = []
        for v in range(V):
            f = zero
            for x in range(3):
                Z[v, x, rows, :] = filter_gain * (Z[v, x, rows, :] + f)
                f = filter_root * (f + PV[v, x + 3, rows, :])
            start.append(f)

        def filter_cells(j, f):
            f = list(f)
            x0 = 3 + j * FILTER_STEP
            for v in range(V):
                w = [PV[v, x0 + u, rows, :] for u in range(FILTER_STEP + 6)]
                for u in range(FILTER_STEP):
                    x = x0 + u
                    Z[v, x, rows, :] = (
                        filter_centre * w[u + 3]
                        + filter_gain * (Z[v, x, rows, :] + f[v])
                        + t1 * (w[u + 4] + w[u + 2])
                        + t2 * (w[u + 5] + w[u + 1])
                        + t3 * (w[u + 6] + w[u])
                    )
                    f[v] = filter_root * (f[v] + w[u + 3])
            return tuple(f)

        f = lax.fori_loop(0, (X - 6) // FILTER_STEP, filter_cells, tuple(start))
        for v in range(V):
            last = f[v]
            for x in range(T, X):
                Z[v, x, rows, :] = filter_gain * (Z[v, x, rows, :] + last)
                last = filter_root * (last + PV[v, x + 3, rows, :])
        return 0

    lax.fori_loop(0, G, filter_rows, 0)

    wait_all(lambda k: ends_copy(E2, G2, s3, r3, k))
    carries(G2, C2, K2, filter_root, s4, r4)

    for c in (*sides, *beyond):
        c.wait()
    block_root = deriv_root**X
    ahead_gain = [-section_b * far * deriv_root**x for x in range(X)]
    behind_gain = [section_b * far * deriv_root ** (X - 1 - x) for x in range(X)]

    def end_rows(yg, _):
        rows = rows_of(yg)
        for v in range(V):
            q = v * G + yg
            left_c = CN[q]
            left_d = E1[lines + q] + block_root * K1[lines + q]
            right_c = E1[q] + block_root * K1[q]
            right_d = DN[q]
            w = []
            for u in range(3):
                w.append(
                    PV[v, u, rows, :]
                    + (ahead_gain[T + u] * left_c + behind_gain[T + u] * left_d)
                )
            w += [PV[v, 3 + u, rows, :] for u in range(6)]
            w2 = [PV[v, X - 3 + u, rows, :] for u in range(6)]
            for u in range(3):
                w2.append(
                    PV[v, X + 3 + u, rows, :]
                    + (ahead_gain[u] * right_c + behind_gain[u] * right_d)
                )
            for x0, w in ((0, w), (T, w2)):
                for u in range(3):
                    Z[v, x0 + u, rows, :] = (
                        Z[v, x0 + u, rows, :]
                        + filter_centre * w[u + 3]
                        + t1 * (w[u + 4] + w[u + 2])
                        + t2 * (w[u + 5] + w[u + 1])
                        + t3 * (w[u + 6] + w[u])
                    )
        return 0

    lax.fori_loop(0, G, end_rows, 0)
    wait_all(lambda k: carry_copy(C2, K2, s4, r4, k))


def last_kernel(z_ref, s_ref, carry_ref, state_h, inc_h, out, sem):
    X = z_ref.shape[1]
    G = z_ref.shape[2] // ROWS
    inc_out = pltpu.make_async_copy(s_ref, inc_h, sem.at[X // LAST_STEP])
    parts = X // LAST_STEP

    def state_out(j):
        planes = pl.ds(j * LAST_STEP, LAST_STEP)
        return pltpu.make_async_copy(out.at[:, planes], state_h.at[:, planes], sem.at[j])

    inc_out.start()
    for j in range(parts):
        for v in range(5):
            for yg in range(G):
                rows = slice(yg * ROWS, yg * ROWS + ROWS)
                ahead = carry_ref[v * G + yg]
                behind = carry_ref[(5 + v) * G + yg]
                for u in range(LAST_STEP):
                    x = j * LAST_STEP + u
                    out[v, x, rows, :] = z_ref[v, x, rows, :] + (
                        (filter_gain * filter_root**x) * ahead
                        + (filter_gain * filter_root ** (X - 1 - x)) * behind
                    )
        state_out(j).start()
    for j in range(parts):
        state_out(j).wait()
    inc_out.wait()


def section(n, zn, density, momentum, energy, increment):
    X, Y, L = density.shape
    G = Y // ROWS
    ends = 2 * 5 * G
    f32 = jnp.float32
    pack = pltpu.VMEM((5, Y, L), f32)
    end = pltpu.VMEM((ends, ROWS, L), f32)
    half = pltpu.VMEM((ends // 2, ROWS, L), f32)
    many = pltpu.SemaphoreType.DMA((n,))
    anywhere = pl.BlockSpec(memory_space=pl.ANY)
    hbm = pl.BlockSpec(memory_space=pltpu.HBM)
    vmem = pl.BlockSpec(memory_space=pltpu.VMEM)
    part, register, carry = pl.pallas_call(
        functools.partial(kernel, n, zn),
        out_shape=(
            OUT((5, X, Y, L), f32),
            OUT((5, X, Y, L), f32),
            OUT((ends, ROWS, L), f32),
        ),
        in_specs=[hbm] * 4,
        out_specs=(vmem,) * 3,
        scratch_shapes=[
            pltpu.VMEM((5, X, Y, L), f32),
            pltpu.VMEM((5, X + 2, Y, L), f32),
            pltpu.VMEM((5, X, Y + 2 * ROWS, L), f32),
            pltpu.VMEM((5, X, Y, L), f32),
            pltpu.VMEM((5, X + 6, Y, L), f32),
            pltpu.VMEM((2 * L, L), jnp.bfloat16),
            pack, pack, pack, pack,
            end, end, end, end, end, end, end,
            pltpu.VMEM((2, 5, 3, Y, L), f32),
            half, half, half,
            pltpu.SemaphoreType.DMA((3, G)),
            pltpu.SemaphoreType.DMA,
            pltpu.SemaphoreType.DMA((10,)),
            pltpu.SemaphoreType.DMA((10,)),
            many, many, many, many, many, many, many, many,
        ],
        compiler_params=pltpu.CompilerParams(
            collective_id=0, has_side_effects=True, vmem_limit_bytes=VLIM * 1024 * 1024
        ),
    )(density, momentum, energy, increment)
    return pl.pallas_call(
        last_kernel,
        out_shape=(
            jax.ShapeDtypeStruct((5, X, Y, L), f32),
            jax.ShapeDtypeStruct((5, X, Y, L), f32),
        ),
        in_specs=[vmem] * 3,
        out_specs=(hbm, hbm),
        scratch_shapes=[
            pltpu.VMEM((5, X, Y, L), f32),
            pltpu.SemaphoreType.DMA((X // LAST_STEP + 1,)),
        ],
        compiler_params=pltpu.CompilerParams(vmem_limit_bytes=16 * 1024 * 1024),
    )(part, register, carry)


def solution(mesh):
    in_specs = (
        P("gx", "gy", "gz"),
        P(None, "gx", "gy", "gz"),
        P("gx", "gy", "gz"),
        P(None, "gx", "gy", "gz"),
    )
    out_specs = (P(None, "gx", "gy", "gz"), P(None, "gx", "gy", "gz"))
    return jax.shard_map(
        functools.partial(section, mesh.shape["gx"], mesh.shape["gz"]),
        mesh=mesh,
        in_specs=in_specs,
        out_specs=out_specs,
        check_vma=False,
    )
```

```python
import functools
import math

import jax
import jax.numpy as jnp
from jax import lax
from jax.experimental import pallas as pl
from jax.experimental.pallas import tpu as pltpu
from jax.sharding import PartitionSpec as P

deriv_alpha = 1.0 / 3.0
filter_alpha = 0.4999
gas_gamma = 1.4
time_step = 0.2
section_a = -5.0 / 9.0
section_b = 15.0 / 16.0
MESH = pl.DeviceIdType.MESH
ROWS = 8
FLUX_STEP = 6
NEAR_STEP = 6
UPDATE_STEP = 6
FILTER_STEP = 6
LAST_STEP = 2
VLIM = 56
YZ_SPLIT = 16
OUT = pltpu.VMEM
LANES = 128


def root_of(coupling):
    return (-1.0 + math.sqrt(1.0 - 4.0 * coupling * coupling)) / (2.0 * coupling)


deriv_root = root_of(deriv_alpha)
deriv_gain = (
    (25.0 / 36.0)
    / math.sqrt(1.0 - 4.0 * deriv_alpha * deriv_alpha)
    * (1.0 / deriv_root - deriv_root)
)
filter_root = root_of(filter_alpha)


def filter_parts(b):
    w = [
        (93.0 + 70.0 * b) / 128.0,
        (7.0 + 18.0 * b) / 16.0,
        (-7.0 + 14.0 * b) / 32.0,
        (1.0 - 2.0 * b) / 16.0,
        (-1.0 + 2.0 * b) / 128.0,
    ]
    c4 = 8 * w[4]
    c3 = 4 * w[3]
    c2 = 2 * w[2] - 8 * w[4]
    c1 = w[1] - 3 * w[3]
    c0 = w[0] - w[2] + w[4]
    q3 = c4 / (2 * b)
    q2 = (c3 - q3) / (2 * b)
    q1 = (c2 - q2) / (2 * b)
    q0 = (c1 - q1) / (2 * b)
    gain = (c0 - q0) / math.sqrt(1.0 - 4.0 * b * b)
    centre = q0 + q2 / 2 + gain
    return centre, (q1 / 2 + 3 * q3 / 8, q2 / 4, q3 / 8), gain


filter_centre, filter_side, filter_gain = filter_parts(filter_alpha)


def kernel(
    n, zn, rho_h, mom_h, en_h, inc_h,
    Z, S, K2,
    U, FX, FY, FZ, PV, B,
    LP, RP, LR, RR,
    E1, G1, C1, K1, E2, G2, C2,
    PE, FT, CN, DN,
    in_sem, inc_sem, halo_s, halo_r,
    s1, r1, s2, r2, s3, r3, s4, r4,
):
    X = U.shape[1]
    Y = U.shape[2]
    G = Y // ROWS
    V = 5
    T = X - 3
    per = E1.shape[0] // n
    order = sorted(range(1, n), key=lambda k: (-min(k % 4, 4 - k % 4) - min(k // 4, 4 - k // 4), k))
    me = lax.axis_index("gx")
    mey = lax.axis_index("gy")
    mez = lax.axis_index("gz")
    right = lax.rem(me + 1, n)
    left = lax.rem(me + n - 1, n)
    other = 1 - mey
    zup = lax.rem(mez + 1, zn)
    zdown = lax.rem(mez + zn - 1, zn)

    def rows_of(yg):
        return pl.ds(pl.multiple_of(yg * ROWS, ROWS), ROWS)

    def group_at(i):
        return lax.rem(i + G - 1, G)

    def loads(i):
        rows = rows_of(group_at(i))
        return (
            pltpu.make_async_copy(rho_h.at[:, rows, :], U.at[0, :, rows, :], in_sem.at[0, i]),
            pltpu.make_async_copy(mom_h.at[:, :, rows, :], U.at[pl.ds(1, 3), :, rows, :], in_sem.at[1, i]),
            pltpu.make_async_copy(en_h.at[:, rows, :], U.at[4, :, rows, :], in_sem.at[2, i]),
        )

    for i in range(G):
        for c in loads(i):
            c.start()
    inc_load = pltpu.make_async_copy(inc_h, S, inc_sem)
    inc_load.start()

    barrier = pltpu.get_barrier_semaphore()

    def greet(k, _):
        pl.semaphore_signal(
            barrier, inc=1, device_id={"gx": lax.rem(me + k, n)}, device_id_type=MESH
        )
        return 0

    lax.fori_loop(1, n, greet, 0)
    pl.semaphore_signal(barrier, inc=1, device_id={"gy": other}, device_id_type=MESH)
    pl.semaphore_signal(barrier, inc=1, device_id={"gz": zup}, device_id_type=MESH)
    pl.semaphore_signal(barrier, inc=1, device_id={"gz": zdown}, device_id_type=MESH)

    lane = lax.broadcasted_iota(jnp.int32, (ROWS, LANES), 1)
    zero = jnp.zeros((ROWS, LANES), jnp.float32)
    zeros = (zero,) * V

    apart = lax.rem(
        lax.broadcasted_iota(jnp.int32, (2 * LANES, LANES), 0)
        + (2 * LANES - lax.broadcasted_iota(jnp.int32, (2 * LANES, LANES), 1)),
        LANES,
    )
    band = jnp.zeros((2 * LANES, LANES), jnp.float32)
    for o, weight in ((1, 45.0), (2, -9.0), (3, 1.0)):
        band = jnp.where(apart == o, weight, band)
        band = jnp.where(apart == LANES - o, -weight, band)
    B[...] = band.astype(jnp.bfloat16)

    def flux_rows(i, _):
        for c in loads(i):
            c.wait()
        yg = group_at(i)
        rows = rows_of(yg)
        rows_y = pl.ds(pl.multiple_of(yg * ROWS + ROWS, ROWS), ROWS)

        def flux_cells(j, carry):
            ef, g, lp, rp, weight = carry
            ef, g, lp, rp = list(ef), list(g), list(lp), list(rp)
            for u in range(FLUX_STEP):
                x = X - 1 - u - j * FLUX_STEP
                rho = U[0, x, rows, :]
                m0 = U[1, x, rows, :]
                m1 = U[2, x, rows, :]
                m2 = U[3, x, rows, :]
                en = U[4, x, rows, :]
                inv = 1.0 / rho
                v0 = m0 * inv
                v1 = m1 * inv
                v2 = m2 * inv
                a00 = m0 * v0
                a11 = m1 * v1
                a22 = m2 * v2
                a01 = m0 * v1
                a02 = m0 * v2
                a12 = m1 * v2
                pressure = (gas_gamma - 1.0) * (en - 0.5 * (a00 + a11 + a22))
                total = en + pressure
                fx = (m0, a00 + pressure, a01, a02, total * v0)
                fy = (m1, a01, a11 + pressure, a12, total * v1)
                fz = (m2, a02, a12, a22 + pressure, total * v2)
                now = jnp.where(x < T, weight, 0.0)
                keep_l = lane < 3 * x + 3
                keep_r = lane < 3 * x + 6
                for v in range(V):
                    FX[v, x + 1, rows, :] = fx[v]
                    FY[v, x, rows_y, :] = fy[v]
                    FZ[v, x, rows, :] = fz[v]
                    Z[v, x, rows, :] = g[v]
                    g[v] = deriv_root * (g[v] + fx[v])
                    ef[v] = ef[v] + now * fx[v]
                    turned = pltpu.roll(fz[v], 3 * x + 3, 1)
                    lp[v] = jnp.where(keep_l, turned, lp[v])
                    rp[v] = jnp.where(keep_r, turned, rp[v])
                weight = jnp.where(x < T, weight * deriv_root, weight)
            return tuple(ef), tuple(g), tuple(lp), tuple(rp), weight

        ef, g, lp, rp, _ = lax.fori_loop(
            0, X // FLUX_STEP, flux_cells,
            (zeros, zeros, zeros, zeros, jnp.float32(deriv_root)),
        )
        for v in range(V):
            FT[v * G + yg] = ef[v]
            f = ef[v]
            for x in range(T, X):
                f = deriv_root * (f + FX[v, x + 1, rows, :])
            E1[v * G + yg] = f
            E1[V * G + v * G + yg] = g[v]
            LP[v, rows, :] = lp[v]
            RP[v, rows, :] = rp[v]
        return 0

    def slot_of(owner, block):
        return jnp.where(owner < n // 2, block, n - 1 - block)

    def chunk(i):
        return pl.ds(i * per, per)

    def ends_copy(E, gathered, ssem, rsem, k):
        owner = lax.rem(me + k, n)
        return pltpu.make_async_remote_copy(
            src_ref=E.at[chunk(owner)],
            dst_ref=gathered.at[chunk(slot_of(owner, me))],
            send_sem=ssem.at[k],
            recv_sem=rsem.at[k],
            device_id={"gx": owner},
            device_id_type=MESH,
        )

    def keep_own(src, dst, start, end):
        for q in range(per):
            dst[end * per + q] = src[start * per + q]

    def send_ends(E, gathered, ssem, rsem):
        for k in order:
            ends_copy(E, gathered, ssem, rsem, k).start()
        keep_own(E, gathered, me, slot_of(me, me))

    def carry_copy(C, K, ssem, rsem, k):
        block = lax.rem(me + k, n)
        return pltpu.make_async_remote_copy(
            src_ref=C.at[chunk(slot_of(me, block))],
            dst_ref=K.at[chunk(me)],
            send_sem=ssem.at[k],
            recv_sem=rsem.at[k],
            device_id={"gx": block},
            device_id_type=MESH,
        )

    def wait_all(make):
        def one(k, _):
            make(k).wait()
            return 0

        lax.fori_loop(1, n, one, 0)

    def carries(gathered, C, K, root, ssem, rsem):
        block_root = root**X
        scale = 1.0 / (1.0 - block_root**n)

        def total(s, h):
            return tuple(gathered[s * per + q] + block_root * h[q] for q in range(per))

        h = lax.fori_loop(0, n, total, (zero,) * per)

        def step(s, c):
            for q in range(per):
                C[s * per + q] = c[q]
            return tuple(gathered[s * per + q] + block_root * c[q] for q in range(per))

        lax.fori_loop(0, n, step, tuple(h[q] * scale for q in range(per)))

        for k in order:
            carry_copy(C, K, ssem, rsem, k).start()
        keep_own(C, K, slot_of(me, me), me)

    def remote(src, dst, i, device):
        return pltpu.make_async_remote_copy(
            src_ref=src, dst_ref=dst, send_sem=halo_s.at[i], recv_sem=halo_r.at[i],
            device_id=device, device_id_type=MESH,
        )

    halo = [
        remote(LP, LR, 0, {"gz": zup}),
        remote(RP, RR, 1, {"gz": zdown}),
        remote(FY.at[:, :, pl.ds(Y, ROWS), :], FY.at[:, :, pl.ds(0, ROWS), :], 2, {"gy": other}),
        remote(FY.at[:, :, pl.ds(ROWS, ROWS), :], FY.at[:, :, pl.ds(Y + ROWS, ROWS), :], 3, {"gy": other}),
        remote(FX.at[:, pl.ds(X, 1)], FX.at[:, pl.ds(0, 1)], 4, {"gx": right}),
        remote(FX.at[:, pl.ds(1, 1)], FX.at[:, pl.ds(X + 1, 1)], 5, {"gx": left}),
    ]
    lax.fori_loop(0, G, flux_rows, 0)
    pl.semaphore_wait(barrier, n + 2)
    send_ends(E1, G1, s1, r1)
    halo[2].start()
    halo[3].start()
    for i in (0, 1, 4, 5):
        halo[i].start()

    inc_load.wait()
    halo[2].wait()
    halo[3].wait()
    k1, k2, k3 = (-time_step * w for w in (0.75, -0.15, 1.0 / 60.0))

    z_scale = -time_step / 60.0

    def yz_plane(i, _):
        x = jnp.where(i < 3, i, jnp.where(i < 6, i + X - 6, i - 3))
        hz = FZ[:, x].reshape(V * Y, LANES)
        head = hz.astype(jnp.bfloat16)
        rest = hz - head.astype(jnp.float32)
        middle = rest.astype(jnp.bfloat16)
        tail = (rest - middle.astype(jnp.float32)).astype(jnp.bfloat16)
        dz = jnp.dot(
            jnp.concatenate([head, middle], axis=1), B[...], preferred_element_type=jnp.float32
        ) + jnp.dot(tail, B[0:LANES, :], preferred_element_type=jnp.float32)
        for v in range(V):
            for yg in range(G):
                base = ROWS + yg * ROWS
                out = slice(yg * ROWS, yg * ROWS + ROWS)
                at = v * Y + yg * ROWS

                def both(o):
                    return (
                        FY[v, x, base + o : base + o + ROWS, :]
                        - FY[v, x, base - o : base - o + ROWS, :]
                    )

                S[v, x, out, :] = (
                    (section_a * S[v, x, out, :] + z_scale * dz[at : at + ROWS, :])
                    + (k1 * both(1) + k2 * both(2) + k3 * both(3))
                )
        return 0

    lax.fori_loop(0, YZ_SPLIT, yz_plane, 0)

    wait_all(lambda k: ends_copy(E1, G1, s1, r1, k))
    carries(G1, C1, K1, deriv_root, s2, r2)

    halo[0].wait()
    halo[1].wait()
    third = lax.rem(lane, 3)
    weights = (k1, k2, k3)

    def z_edges(v, _):
        for yg in range(G):
            rows = slice(yg * ROWS, yg * ROWS + ROWS)
            dl = LR[v, rows, :] - LP[v, rows, :]
            dr = RR[v, rows, :] - RP[v, rows, :]
            low = zero
            high = zero
            for o in (1, 2, 3):
                low = low - jnp.where(third < o, weights[o - 1] * pltpu.roll(dl, o, 1), 0.0)
                high = high + jnp.where(
                    third >= 3 - o, weights[o - 1] * pltpu.roll(dr, LANES - o, 1), 0.0
                )
            LR[v, rows, :] = low
            RR[v, rows, :] = high
        return 0

    lax.fori_loop(0, V, z_edges, 0)

    halo[4].wait()
    halo[5].wait()
    near = -time_step / 12.0
    far = -time_step * deriv_gain
    rim = (lane < 3) | (lane >= LANES - 3)

    def near_cells(rows, v, x0, count, f, low, high):
        window = [FX[v, x0 + u, rows, :] for u in range(count + 2)]
        out = []
        for u in range(count):
            x = x0 + u
            edge = jnp.where(lane < 3 * x + 3, high, low)
            edge = jnp.where(rim, pltpu.roll(edge, 125 - 3 * x, 1), 0.0)
            s = (
                (S[v, x, rows, :] + edge)
                + near * (window[u + 2] - window[u])
                + far * (Z[v, x, rows, :] - f)
            )
            S[v, x, rows, :] = s
            out.append(s)
            f = deriv_root * (f + window[u + 1])
        return f, out

    def outer_rows(yg, _):
        rows = rows_of(yg)
        for v in range(V):
            low = LR[v, rows, :]
            high = RR[v, rows, :]
            for side, x0, f in ((0, T, FT[v * G + yg]), (1, 0, zero)):
                _, found = near_cells(rows, v, x0, 3, f, low, high)
                for u in range(3):
                    PE[side, v, u, rows, :] = U[v, x0 + u, rows, :] + section_b * found[u]
        return 0

    lax.fori_loop(0, G, outer_rows, 0)
    sides = [
        remote(PE.at[0], PV.at[:, pl.ds(0, 3)], 6, {"gx": right}),
        remote(PE.at[1], PV.at[:, pl.ds(X + 3, 3)], 7, {"gx": left}),
    ]
    sides[0].start()
    sides[1].start()
    lax.fori_loop(YZ_SPLIT, X, yz_plane, 0)

    def near_rows(yg, _):
        rows = rows_of(yg)
        low = [LR[v, rows, :] for v in range(V)]
        high = [RR[v, rows, :] for v in range(V)]
        start = []
        for v in range(V):
            f = zero
            for x in range(3):
                f = deriv_root * (f + FX[v, x + 1, rows, :])
            start.append(f)

        def cells(j, f):
            x0 = 3 + j * NEAR_STEP
            return tuple(
                near_cells(rows, v, x0, NEAR_STEP, f[v], low[v], high[v])[0] for v in range(V)
            )

        lax.fori_loop(0, (X - 6) // NEAR_STEP, cells, tuple(start))
        return 0

    lax.fori_loop(0, G, near_rows, 0)

    wait_all(lambda k: carry_copy(C1, K1, s2, r2, k))
    lines = V * G
    beyond = [
        remote(K1.at[pl.ds(0, lines)], CN, 8, {"gx": right}),
        remote(K1.at[pl.ds(lines, lines)], DN, 9, {"gx": left}),
    ]

    def update_rows(yg, _):
        rows = rows_of(yg)
        cf = [(-far * deriv_root ** (X - 1)) * K1[v * G + yg] for v in range(V)]
        cb = [far * K1[V * G + v * G + yg] for v in range(V)]

        def update_cells(j, carry):
            ef, g, wf, wb, weight = carry
            ef, g = list(ef), list(g)
            for u in range(UPDATE_STEP):
                x = X - 1 - u - j * UPDATE_STEP
                for v in range(V):
                    s = S[v, x, rows, :] + (wf * cf[v] + wb * cb[v])
                    p = U[v, x, rows, :] + section_b * s
                    S[v, x, rows, :] = s
                    PV[v, x + 3, rows, :] = p
                    Z[v, x, rows, :] = g[v]
                    g[v] = filter_root * (g[v] + p)
                    ef[v] = ef[v] + weight * p
                wf = wf * (1.0 / deriv_root)
                wb = wb * deriv_root
                weight = weight * filter_root
            return tuple(ef), tuple(g), wf, wb, weight

        ef, g, _, _, _ = lax.fori_loop(
            0, X // UPDATE_STEP, update_cells,
            (zeros, zeros, jnp.float32(1.0), jnp.float32(1.0), jnp.float32(filter_root)),
        )
        for v in range(V):
            E2[v * G + yg] = ef[v]
            E2[V * G + v * G + yg] = g[v]
        return 0

    lax.fori_loop(0, G, update_rows, 0)

    send_ends(E2, G2, s3, r3)
    beyond[0].start()
    beyond[1].start()
    t1, t2, t3 = filter_side

    def filter_rows(yg, _):
        rows = rows_of(yg)
        start = []
        for v in range(V):
            f = zero
            for x in range(3):
                Z[v, x, rows, :] = filter_gain * (Z[v, x, rows, :] + f)
                f = filter_root * (f + PV[v, x + 3, rows, :])
            start.append(f)

        def filter_cells(j, f):
            f = list(f)
            x0 = 3 + j * FILTER_STEP
            for v in range(V):
                w = [PV[v, x0 + u, rows, :] for u in range(FILTER_STEP + 6)]
                for u in range(FILTER_STEP):
                    x = x0 + u
                    Z[v, x, rows, :] = (
                        filter_centre * w[u + 3]
                        + filter_gain * (Z[v, x, rows, :] + f[v])
                        + t1 * (w[u + 4] + w[u + 2])
                        + t2 * (w[u + 5] + w[u + 1])
                        + t3 * (w[u + 6] + w[u])
                    )
                    f[v] = filter_root * (f[v] + w[u + 3])
            return tuple(f)

        f = lax.fori_loop(0, (X - 6) // FILTER_STEP, filter_cells, tuple(start))
        for v in range(V):
            last = f[v]
            for x in range(T, X):
                Z[v, x, rows, :] = filter_gain * (Z[v, x, rows, :] + last)
                last = filter_root * (last + PV[v, x + 3, rows, :])
        return 0

    lax.fori_loop(0, G, filter_rows, 0)

    wait_all(lambda k: ends_copy(E2, G2, s3, r3, k))
    carries(G2, C2, K2, filter_root, s4, r4)

    for c in (*sides, *beyond):
        c.wait()
    block_root = deriv_root**X
    ahead_gain = [-section_b * far * deriv_root**x for x in range(X)]
    behind_gain = [section_b * far * deriv_root ** (X - 1 - x) for x in range(X)]

    def end_rows(yg, _):
        rows = rows_of(yg)
        for v in range(V):
            q = v * G + yg
            left_c = CN[q]
            left_d = E1[lines + q] + block_root * K1[lines + q]
            right_c = E1[q] + block_root * K1[q]
            right_d = DN[q]
            w = []
            for u in range(3):
                w.append(
                    PV[v, u, rows, :]
                    + (ahead_gain[T + u] * left_c + behind_gain[T + u] * left_d)
                )
            w += [PV[v, 3 + u, rows, :] for u in range(6)]
            w2 = [PV[v, X - 3 + u, rows, :] for u in range(6)]
            for u in range(3):
                w2.append(
                    PV[v, X + 3 + u, rows, :]
                    + (ahead_gain[u] * right_c + behind_gain[u] * right_d)
                )
            for x0, w in ((0, w), (T, w2)):
                for u in range(3):
                    Z[v, x0 + u, rows, :] = (
                        Z[v, x0 + u, rows, :]
                        + filter_centre * w[u + 3]
                        + t1 * (w[u + 4] + w[u + 2])
                        + t2 * (w[u + 5] + w[u + 1])
                        + t3 * (w[u + 6] + w[u])
                    )
        return 0

    lax.fori_loop(0, G, end_rows, 0)
    wait_all(lambda k: carry_copy(C2, K2, s4, r4, k))


def last_kernel(z_ref, s_ref, carry_ref, state_h, inc_h, out, sem):
    X = z_ref.shape[1]
    G = z_ref.shape[2] // ROWS
    inc_out = pltpu.make_async_copy(s_ref, inc_h, sem.at[X // LAST_STEP])
    parts = X // LAST_STEP

    def state_out(j):
        planes = pl.ds(j * LAST_STEP, LAST_STEP)
        return pltpu.make_async_copy(out.at[:, planes], state_h.at[:, planes], sem.at[j])

    inc_out.start()
    for j in range(parts):
        for v in range(5):
            for yg in range(G):
                rows = slice(yg * ROWS, yg * ROWS + ROWS)
                ahead = carry_ref[v * G + yg]
                behind = carry_ref[(5 + v) * G + yg]
                for u in range(LAST_STEP):
                    x = j * LAST_STEP + u
                    out[v, x, rows, :] = z_ref[v, x, rows, :] + (
                        (filter_gain * filter_root**x) * ahead
                        + (filter_gain * filter_root ** (X - 1 - x)) * behind
                    )
        state_out(j).start()
    for j in range(parts):
        state_out(j).wait()
    inc_out.wait()


def section(n, zn, density, momentum, energy, increment):
    X, Y, L = density.shape
    G = Y // ROWS
    ends = 2 * 5 * G
    f32 = jnp.float32
    pack = pltpu.VMEM((5, Y, L), f32)
    end = pltpu.VMEM((ends, ROWS, L), f32)
    half = pltpu.VMEM((ends // 2, ROWS, L), f32)
    many = pltpu.SemaphoreType.DMA((n,))
    anywhere = pl.BlockSpec(memory_space=pl.ANY)
    hbm = pl.BlockSpec(memory_space=pltpu.HBM)
    vmem = pl.BlockSpec(memory_space=pltpu.VMEM)
    part, register, carry = pl.pallas_call(
        functools.partial(kernel, n, zn),
        out_shape=(
            OUT((5, X, Y, L), f32),
            OUT((5, X, Y, L), f32),
            OUT((ends, ROWS, L), f32),
        ),
        in_specs=[hbm] * 4,
        out_specs=(vmem,) * 3,
        scratch_shapes=[
            pltpu.VMEM((5, X, Y, L), f32),
            pltpu.VMEM((5, X + 2, Y, L), f32),
            pltpu.VMEM((5, X, Y + 2 * ROWS, L), f32),
            pltpu.VMEM((5, X, Y, L), f32),
            pltpu.VMEM((5, X + 6, Y, L), f32),
            pltpu.VMEM((2 * L, L), jnp.bfloat16),
            pack, pack, pack, pack,
            end, end, end, end, end, end, end,
            pltpu.VMEM((2, 5, 3, Y, L), f32),
            half, half, half,
            pltpu.SemaphoreType.DMA((3, G)),
            pltpu.SemaphoreType.DMA,
            pltpu.SemaphoreType.DMA((10,)),
            pltpu.SemaphoreType.DMA((10,)),
            many, many, many, many, many, many, many, many,
        ],
        compiler_params=pltpu.CompilerParams(
            collective_id=0, has_side_effects=True, vmem_limit_bytes=VLIM * 1024 * 1024
        ),
    )(density, momentum, energy, increment)
    return pl.pallas_call(
        last_kernel,
        out_shape=(
            jax.ShapeDtypeStruct((5, X, Y, L), f32),
            jax.ShapeDtypeStruct((5, X, Y, L), f32),
        ),
        in_specs=[vmem] * 3,
        out_specs=(hbm, hbm),
        scratch_shapes=[
            pltpu.VMEM((5, X, Y, L), f32),
            pltpu.SemaphoreType.DMA((X // LAST_STEP + 1,)),
        ],
        compiler_params=pltpu.CompilerParams(vmem_limit_bytes=16 * 1024 * 1024),
    )(part, register, carry)


def solution(mesh):
    in_specs = (
        P("gx", "gy", "gz"),
        P(None, "gx", "gy", "gz"),
        P("gx", "gy", "gz"),
        P(None, "gx", "gy", "gz"),
    )
    out_specs = (P(None, "gx", "gy", "gz"), P(None, "gx", "gy", "gz"))
    return jax.shard_map(
        functools.partial(section, mesh.shape["gx"], mesh.shape["gz"]),
        mesh=mesh,
        in_specs=in_specs,
        out_specs=out_specs,
        check_vma=False,
    )
```

```python
import functools
import math

import jax
import jax.numpy as jnp
from jax import lax
from jax.experimental import pallas as pl
from jax.experimental.pallas import tpu as pltpu
from jax.sharding import PartitionSpec as P

deriv_alpha = 1.0 / 3.0
filter_alpha = 0.4999
gas_gamma = 1.4
time_step = 0.2
section_a = -5.0 / 9.0
section_b = 15.0 / 16.0
MESH = pl.DeviceIdType.MESH
ROWS = 8
FLUX_STEP = 8
NEAR_STEP = 6
UPDATE_STEP = 8
FILTER_STEP = 6
LAST_STEP = 2
VLIM = 56
YZ_SPLIT = 16
OUT = pltpu.VMEM
LANES = 128


def root_of(coupling):
    return (-1.0 + math.sqrt(1.0 - 4.0 * coupling * coupling)) / (2.0 * coupling)


deriv_root = root_of(deriv_alpha)
deriv_gain = (
    (25.0 / 36.0)
    / math.sqrt(1.0 - 4.0 * deriv_alpha * deriv_alpha)
    * (1.0 / deriv_root - deriv_root)
)
filter_root = root_of(filter_alpha)


def filter_parts(b):
    w = [
        (93.0 + 70.0 * b) / 128.0,
        (7.0 + 18.0 * b) / 16.0,
        (-7.0 + 14.0 * b) / 32.0,
        (1.0 - 2.0 * b) / 16.0,
        (-1.0 + 2.0 * b) / 128.0,
    ]
    c4 = 8 * w[4]
    c3 = 4 * w[3]
    c2 = 2 * w[2] - 8 * w[4]
    c1 = w[1] - 3 * w[3]
    c0 = w[0] - w[2] + w[4]
    q3 = c4 / (2 * b)
    q2 = (c3 - q3) / (2 * b)
    q1 = (c2 - q2) / (2 * b)
    q0 = (c1 - q1) / (2 * b)
    gain = (c0 - q0) / math.sqrt(1.0 - 4.0 * b * b)
    centre = q0 + q2 / 2 + gain
    return centre, (q1 / 2 + 3 * q3 / 8, q2 / 4, q3 / 8), gain


filter_centre, filter_side, filter_gain = filter_parts(filter_alpha)


def kernel(
    n, zn, rho_h, mom_h, en_h, inc_h,
    Z, S, K2,
    U, FX, FY, FZ, PV, B,
    LP, RP, LR, RR,
    E1, G1, C1, K1, E2, G2, C2,
    PE, FT, CN, DN,
    in_sem, inc_sem, halo_s, halo_r,
    s1, r1, s2, r2, s3, r3, s4, r4,
):
    X = U.shape[1]
    Y = U.shape[2]
    G = Y // ROWS
    V = 5
    T = X - 3
    per = E1.shape[0] // n
    order = sorted(range(1, n), key=lambda k: (-min(k % 4, 4 - k % 4) - min(k // 4, 4 - k // 4), k))
    me = lax.axis_index("gx")
    mey = lax.axis_index("gy")
    mez = lax.axis_index("gz")
    right = lax.rem(me + 1, n)
    left = lax.rem(me + n - 1, n)
    other = 1 - mey
    zup = lax.rem(mez + 1, zn)
    zdown = lax.rem(mez + zn - 1, zn)

    def rows_of(yg):
        return pl.ds(pl.multiple_of(yg * ROWS, ROWS), ROWS)

    def group_at(i):
        return lax.rem(i + G - 1, G)

    def loads(i):
        rows = rows_of(group_at(i))
        return (
            pltpu.make_async_copy(rho_h.at[:, rows, :], U.at[0, :, rows, :], in_sem.at[0, i]),
            pltpu.make_async_copy(mom_h.at[:, :, rows, :], U.at[pl.ds(1, 3), :, rows, :], in_sem.at[1, i]),
            pltpu.make_async_copy(en_h.at[:, rows, :], U.at[4, :, rows, :], in_sem.at[2, i]),
        )

    for i in range(G):
        for c in loads(i):
            c.start()
    inc_load = pltpu.make_async_copy(inc_h, S, inc_sem)
    inc_load.start()

    barrier = pltpu.get_barrier_semaphore()

    def greet(k, _):
        pl.semaphore_signal(
            barrier, inc=1, device_id={"gx": lax.rem(me + k, n)}, device_id_type=MESH
        )
        return 0

    lax.fori_loop(1, n, greet, 0)
    pl.semaphore_signal(barrier, inc=1, device_id={"gy": other}, device_id_type=MESH)
    pl.semaphore_signal(barrier, inc=1, device_id={"gz": zup}, device_id_type=MESH)
    pl.semaphore_signal(barrier, inc=1, device_id={"gz": zdown}, device_id_type=MESH)

    lane = lax.broadcasted_iota(jnp.int32, (ROWS, LANES), 1)
    zero = jnp.zeros((ROWS, LANES), jnp.float32)
    zeros = (zero,) * V

    apart = lax.rem(
        lax.broadcasted_iota(jnp.int32, (2 * LANES, LANES), 0)
        + (2 * LANES - lax.broadcasted_iota(jnp.int32, (2 * LANES, LANES), 1)),
        LANES,
    )
    band = jnp.zeros((2 * LANES, LANES), jnp.float32)
    for o, weight in ((1, 45.0), (2, -9.0), (3, 1.0)):
        band = jnp.where(apart == o, weight, band)
        band = jnp.where(apart == LANES - o, -weight, band)
    B[...] = band.astype(jnp.bfloat16)

    def flux_rows(i, _):
        for c in loads(i):
            c.wait()
        yg = group_at(i)
        rows = rows_of(yg)
        rows_y = pl.ds(pl.multiple_of(yg * ROWS + ROWS, ROWS), ROWS)

        def flux_cells(j, carry):
            ef, g, lp, rp, weight = carry
            ef, g, lp, rp = list(ef), list(g), list(lp), list(rp)
            for u in range(FLUX_STEP):
                x = X - 1 - u - j * FLUX_STEP
                rho = U[0, x, rows, :]
                m0 = U[1, x, rows, :]
                m1 = U[2, x, rows, :]
                m2 = U[3, x, rows, :]
                en = U[4, x, rows, :]
                inv = 1.0 / rho
                v0 = m0 * inv
                v1 = m1 * inv
                v2 = m2 * inv
                a00 = m0 * v0
                a11 = m1 * v1
                a22 = m2 * v2
                a01 = m0 * v1
                a02 = m0 * v2
                a12 = m1 * v2
                pressure = (gas_gamma - 1.0) * (en - 0.5 * (a00 + a11 + a22))
                total = en + pressure
                fx = (m0, a00 + pressure, a01, a02, total * v0)
                fy = (m1, a01, a11 + pressure, a12, total * v1)
                fz = (m2, a02, a12, a22 + pressure, total * v2)
                now = jnp.where(x < T, weight, 0.0)
                keep_l = lane < 3 * x + 3
                keep_r = lane < 3 * x + 6
                for v in range(V):
                    FX[v, x + 1, rows, :] = fx[v]
                    FY[v, x, rows_y, :] = fy[v]
                    FZ[v, x, rows, :] = fz[v]
                    Z[v, x, rows, :] = g[v]
                    g[v] = deriv_root * (g[v] + fx[v])
                    ef[v] = ef[v] + now * fx[v]
                    turned = pltpu.roll(fz[v], 3 * x + 3, 1)
                    lp[v] = jnp.where(keep_l, turned, lp[v])
                    rp[v] = jnp.where(keep_r, turned, rp[v])
                weight = jnp.where(x < T, weight * deriv_root, weight)
            return tuple(ef), tuple(g), tuple(lp), tuple(rp), weight

        ef, g, lp, rp, _ = lax.fori_loop(
            0, X // FLUX_STEP, flux_cells,
            (zeros, zeros, zeros, zeros, jnp.float32(deriv_root)),
        )
        for v in range(V):
            FT[v * G + yg] = ef[v]
            f = ef[v]
            for x in range(T, X):
                f = deriv_root * (f + FX[v, x + 1, rows, :])
            E1[v * G + yg] = f
            E1[V * G + v * G + yg] = g[v]
            LP[v, rows, :] = lp[v]
            RP[v, rows, :] = rp[v]
        return 0

    def slot_of(owner, block):
        return jnp.where(owner < n // 2, block, n - 1 - block)

    def chunk(i):
        return pl.ds(i * per, per)

    def ends_copy(E, gathered, ssem, rsem, k):
        owner = lax.rem(me + k, n)
        return pltpu.make_async_remote_copy(
            src_ref=E.at[chunk(owner)],
            dst_ref=gathered.at[chunk(slot_of(owner, me))],
            send_sem=ssem.at[k],
            recv_sem=rsem.at[k],
            device_id={"gx": owner},
            device_id_type=MESH,
        )

    def keep_own(src, dst, start, end):
        for q in range(per):
            dst[end * per + q] = src[start * per + q]

    def send_ends(E, gathered, ssem, rsem):
        for k in order:
            ends_copy(E, gathered, ssem, rsem, k).start()
        keep_own(E, gathered, me, slot_of(me, me))

    def carry_copy(C, K, ssem, rsem, k):
        block = lax.rem(me + k, n)
        return pltpu.make_async_remote_copy(
            src_ref=C.at[chunk(slot_of(me, block))],
            dst_ref=K.at[chunk(me)],
            send_sem=ssem.at[k],
            recv_sem=rsem.at[k],
            device_id={"gx": block},
            device_id_type=MESH,
        )

    def wait_all(make):
        def one(k, _):
            make(k).wait()
            return 0

        lax.fori_loop(1, n, one, 0)

    def carries(gathered, C, K, root, ssem, rsem):
        block_root = root**X
        scale = 1.0 / (1.0 - block_root**n)

        def total(s, h):
            return tuple(gathered[s * per + q] + block_root * h[q] for q in range(per))

        h = lax.fori_loop(0, n, total, (zero,) * per)

        def step(s, c):
            for q in range(per):
                C[s * per + q] = c[q]
            return tuple(gathered[s * per + q] + block_root * c[q] for q in range(per))

        lax.fori_loop(0, n, step, tuple(h[q] * scale for q in range(per)))

        for k in order:
            carry_copy(C, K, ssem, rsem, k).start()
        keep_own(C, K, slot_of(me, me), me)

    def remote(src, dst, i, device):
        return pltpu.make_async_remote_copy(
            src_ref=src, dst_ref=dst, send_sem=halo_s.at[i], recv_sem=halo_r.at[i],
            device_id=device, device_id_type=MESH,
        )

    halo = [
        remote(LP, LR, 0, {"gz": zup}),
        remote(RP, RR, 1, {"gz": zdown}),
        remote(FY.at[:, :, pl.ds(Y, ROWS), :], FY.at[:, :, pl.ds(0, ROWS), :], 2, {"gy": other}),
        remote(FY.at[:, :, pl.ds(ROWS, ROWS), :], FY.at[:, :, pl.ds(Y + ROWS, ROWS), :], 3, {"gy": other}),
        remote(FX.at[:, pl.ds(X, 1)], FX.at[:, pl.ds(0, 1)], 4, {"gx": right}),
        remote(FX.at[:, pl.ds(1, 1)], FX.at[:, pl.ds(X + 1, 1)], 5, {"gx": left}),
    ]
    lax.fori_loop(0, G, flux_rows, 0)
    pl.semaphore_wait(barrier, n + 2)
    send_ends(E1, G1, s1, r1)
    halo[2].start()
    halo[3].start()
    for i in (0, 1, 4, 5):
        halo[i].start()

    inc_load.wait()
    halo[2].wait()
    halo[3].wait()
    k1, k2, k3 = (-time_step * w for w in (0.75, -0.15, 1.0 / 60.0))

    z_scale = -time_step / 60.0

    def yz_plane(i, _):
        x = jnp.where(i < 3, i, jnp.where(i < 6, i + X - 6, i - 3))
        hz = FZ[:, x].reshape(V * Y, LANES)
        head = hz.astype(jnp.bfloat16)
        rest = hz - head.astype(jnp.float32)
        middle = rest.astype(jnp.bfloat16)
        tail = (rest - middle.astype(jnp.float32)).astype(jnp.bfloat16)
        dz = jnp.dot(
            jnp.concatenate([head, middle], axis=1), B[...], preferred_element_type=jnp.float32
        ) + jnp.dot(tail, B[0:LANES, :], preferred_element_type=jnp.float32)
        for v in range(V):
            for yg in range(G):
                base = ROWS + yg * ROWS
                out = slice(yg * ROWS, yg * ROWS + ROWS)
                at = v * Y + yg * ROWS

                def both(o):
                    return (
                        FY[v, x, base + o : base + o + ROWS, :]
                        - FY[v, x, base - o : base - o + ROWS, :]
                    )

                S[v, x, out, :] = (
                    (section_a * S[v, x, out, :] + z_scale * dz[at : at + ROWS, :])
                    + (k1 * both(1) + k2 * both(2) + k3 * both(3))
                )
        return 0

    lax.fori_loop(0, YZ_SPLIT, yz_plane, 0)

    wait_all(lambda k: ends_copy(E1, G1, s1, r1, k))
    carries(G1, C1, K1, deriv_root, s2, r2)

    halo[0].wait()
    halo[1].wait()
    third = lax.rem(lane, 3)
    weights = (k1, k2, k3)

    def z_edges(v, _):
        for yg in range(G):
            rows = slice(yg * ROWS, yg * ROWS + ROWS)
            dl = LR[v, rows, :] - LP[v, rows, :]
            dr = RR[v, rows, :] - RP[v, rows, :]
            low = zero
            high = zero
            for o in (1, 2, 3):
                low = low - jnp.where(third < o, weights[o - 1] * pltpu.roll(dl, o, 1), 0.0)
                high = high + jnp.where(
                    third >= 3 - o, weights[o - 1] * pltpu.roll(dr, LANES - o, 1), 0.0
                )
            LR[v, rows, :] = low
            RR[v, rows, :] = high
        return 0

    lax.fori_loop(0, V, z_edges, 0)

    halo[4].wait()
    halo[5].wait()
    near = -time_step / 12.0
    far = -time_step * deriv_gain
    rim = (lane < 3) | (lane >= LANES - 3)

    def near_cells(rows, v, x0, count, f, low, high):
        window = [FX[v, x0 + u, rows, :] for u in range(count + 2)]
        out = []
        for u in range(count):
            x = x0 + u
            edge = jnp.where(lane < 3 * x + 3, high, low)
            edge = jnp.where(rim, pltpu.roll(edge, 125 - 3 * x, 1), 0.0)
            s = (
                (S[v, x, rows, :] + edge)
                + near * (window[u + 2] - window[u])
                + far * (Z[v, x, rows, :] - f)
            )
            S[v, x, rows, :] = s
            out.append(s)
            f = deriv_root * (f + window[u + 1])
        return f, out

    def outer_rows(yg, _):
        rows = rows_of(yg)
        for v in range(V):
            low = LR[v, rows, :]
            high = RR[v, rows, :]
            for side, x0, f in ((0, T, FT[v * G + yg]), (1, 0, zero)):
                _, found = near_cells(rows, v, x0, 3, f, low, high)
                for u in range(3):
                    PE[side, v, u, rows, :] = U[v, x0 + u, rows, :] + section_b * found[u]
        return 0

    lax.fori_loop(0, G, outer_rows, 0)
    sides = [
        remote(PE.at[0], PV.at[:, pl.ds(0, 3)], 6, {"gx": right}),
        remote(PE.at[1], PV.at[:, pl.ds(X + 3, 3)], 7, {"gx": left}),
    ]
    sides[0].start()
    sides[1].start()
    lax.fori_loop(YZ_SPLIT, X, yz_plane, 0)

    def near_rows(yg, _):
        rows = rows_of(yg)
        low = [LR[v, rows, :] for v in range(V)]
        high = [RR[v, rows, :] for v in range(V)]
        start = []
        for v in range(V):
            f = zero
            for x in range(3):
                f = deriv_root * (f + FX[v, x + 1, rows, :])
            start.append(f)

        def cells(j, f):
            x0 = 3 + j * NEAR_STEP
            return tuple(
                near_cells(rows, v, x0, NEAR_STEP, f[v], low[v], high[v])[0] for v in range(V)
            )

        lax.fori_loop(0, (X - 6) // NEAR_STEP, cells, tuple(start))
        return 0

    lax.fori_loop(0, G, near_rows, 0)

    wait_all(lambda k: carry_copy(C1, K1, s2, r2, k))
    lines = V * G
    beyond = [
        remote(K1.at[pl.ds(0, lines)], CN, 8, {"gx": right}),
        remote(K1.at[pl.ds(lines, lines)], DN, 9, {"gx": left}),
    ]

    def update_rows(yg, _):
        rows = rows_of(yg)
        cf = [(-far * deriv_root ** (X - 1)) * K1[v * G + yg] for v in range(V)]
        cb = [far * K1[V * G + v * G + yg] for v in range(V)]

        def update_cells(j, carry):
            ef, g, wf, wb, weight = carry
            ef, g = list(ef), list(g)
            for u in range(UPDATE_STEP):
                x = X - 1 - u - j * UPDATE_STEP
                for v in range(V):
                    s = S[v, x, rows, :] + (wf * cf[v] + wb * cb[v])
                    p = U[v, x, rows, :] + section_b * s
                    S[v, x, rows, :] = s
                    PV[v, x + 3, rows, :] = p
                    Z[v, x, rows, :] = g[v]
                    g[v] = filter_root * (g[v] + p)
                    ef[v] = ef[v] + weight * p
                wf = wf * (1.0 / deriv_root)
                wb = wb * deriv_root
                weight = weight * filter_root
            return tuple(ef), tuple(g), wf, wb, weight

        ef, g, _, _, _ = lax.fori_loop(
            0, X // UPDATE_STEP, update_cells,
            (zeros, zeros, jnp.float32(1.0), jnp.float32(1.0), jnp.float32(filter_root)),
        )
        for v in range(V):
            E2[v * G + yg] = ef[v]
            E2[V * G + v * G + yg] = g[v]
        return 0

    lax.fori_loop(0, G, update_rows, 0)

    send_ends(E2, G2, s3, r3)
    beyond[0].start()
    beyond[1].start()
    t1, t2, t3 = filter_side

    def filter_rows(yg, _):
        rows = rows_of(yg)
        start = []
        for v in range(V):
            f = zero
            for x in range(3):
                Z[v, x, rows, :] = filter_gain * (Z[v, x, rows, :] + f)
                f = filter_root * (f + PV[v, x + 3, rows, :])
            start.append(f)

        def filter_cells(j, f):
            f = list(f)
            x0 = 3 + j * FILTER_STEP
            for v in range(V):
                w = [PV[v, x0 + u, rows, :] for u in range(FILTER_STEP + 6)]
                for u in range(FILTER_STEP):
                    x = x0 + u
                    Z[v, x, rows, :] = (
                        filter_centre * w[u + 3]
                        + filter_gain * (Z[v, x, rows, :] + f[v])
                        + t1 * (w[u + 4] + w[u + 2])
                        + t2 * (w[u + 5] + w[u + 1])
                        + t3 * (w[u + 6] + w[u])
                    )
                    f[v] = filter_root * (f[v] + w[u + 3])
            return tuple(f)

        f = lax.fori_loop(0, (X - 6) // FILTER_STEP, filter_cells, tuple(start))
        for v in range(V):
            last = f[v]
            for x in range(T, X):
                Z[v, x, rows, :] = filter_gain * (Z[v, x, rows, :] + last)
                last = filter_root * (last + PV[v, x + 3, rows, :])
        return 0

    lax.fori_loop(0, G, filter_rows, 0)

    wait_all(lambda k: ends_copy(E2, G2, s3, r3, k))
    carries(G2, C2, K2, filter_root, s4, r4)

    for c in (*sides, *beyond):
        c.wait()
    block_root = deriv_root**X
    ahead_gain = [-section_b * far * deriv_root**x for x in range(X)]
    behind_gain = [section_b * far * deriv_root ** (X - 1 - x) for x in range(X)]

    def end_rows(yg, _):
        rows = rows_of(yg)
        for v in range(V):
            q = v * G + yg
            left_c = CN[q]
            left_d = E1[lines + q] + block_root * K1[lines + q]
            right_c = E1[q] + block_root * K1[q]
            right_d = DN[q]
            w = []
            for u in range(3):
                w.append(
                    PV[v, u, rows, :]
                    + (ahead_gain[T + u] * left_c + behind_gain[T + u] * left_d)
                )
            w += [PV[v, 3 + u, rows, :] for u in range(6)]
            w2 = [PV[v, X - 3 + u, rows, :] for u in range(6)]
            for u in range(3):
                w2.append(
                    PV[v, X + 3 + u, rows, :]
                    + (ahead_gain[u] * right_c + behind_gain[u] * right_d)
                )
            for x0, w in ((0, w), (T, w2)):
                for u in range(3):
                    Z[v, x0 + u, rows, :] = (
                        Z[v, x0 + u, rows, :]
                        + filter_centre * w[u + 3]
                        + t1 * (w[u + 4] + w[u + 2])
                        + t2 * (w[u + 5] + w[u + 1])
                        + t3 * (w[u + 6] + w[u])
                    )
        return 0

    lax.fori_loop(0, G, end_rows, 0)
    wait_all(lambda k: carry_copy(C2, K2, s4, r4, k))


def last_kernel(z_ref, s_ref, carry_ref, state_h, inc_h, out, sem):
    X = z_ref.shape[1]
    G = z_ref.shape[2] // ROWS
    inc_out = pltpu.make_async_copy(s_ref, inc_h, sem.at[X // LAST_STEP])
    parts = X // LAST_STEP

    def state_out(j):
        planes = pl.ds(j * LAST_STEP, LAST_STEP)
        return pltpu.make_async_copy(out.at[:, planes], state_h.at[:, planes], sem.at[j])

    inc_out.start()
    for j in range(parts):
        for v in range(5):
            for yg in range(G):
                rows = slice(yg * ROWS, yg * ROWS + ROWS)
                ahead = carry_ref[v * G + yg]
                behind = carry_ref[(5 + v) * G + yg]
                for u in range(LAST_STEP):
                    x = j * LAST_STEP + u
                    out[v, x, rows, :] = z_ref[v, x, rows, :] + (
                        (filter_gain * filter_root**x) * ahead
                        + (filter_gain * filter_root ** (X - 1 - x)) * behind
                    )
        state_out(j).start()
    for j in range(parts):
        state_out(j).wait()
    inc_out.wait()


def section(n, zn, density, momentum, energy, increment):
    X, Y, L = density.shape
    G = Y // ROWS
    ends = 2 * 5 * G
    f32 = jnp.float32
    pack = pltpu.VMEM((5, Y, L), f32)
    end = pltpu.VMEM((ends, ROWS, L), f32)
    half = pltpu.VMEM((ends // 2, ROWS, L), f32)
    many = pltpu.SemaphoreType.DMA((n,))
    anywhere = pl.BlockSpec(memory_space=pl.ANY)
    hbm = pl.BlockSpec(memory_space=pltpu.HBM)
    vmem = pl.BlockSpec(memory_space=pltpu.VMEM)
    part, register, carry = pl.pallas_call(
        functools.partial(kernel, n, zn),
        out_shape=(
            OUT((5, X, Y, L), f32),
            OUT((5, X, Y, L), f32),
            OUT((ends, ROWS, L), f32),
        ),
        in_specs=[hbm] * 4,
        out_specs=(vmem,) * 3,
        scratch_shapes=[
            pltpu.VMEM((5, X, Y, L), f32),
            pltpu.VMEM((5, X + 2, Y, L), f32),
            pltpu.VMEM((5, X, Y + 2 * ROWS, L), f32),
            pltpu.VMEM((5, X, Y, L), f32),
            pltpu.VMEM((5, X + 6, Y, L), f32),
            pltpu.VMEM((2 * L, L), jnp.bfloat16),
            pack, pack, pack, pack,
            end, end, end, end, end, end, end,
            pltpu.VMEM((2, 5, 3, Y, L), f32),
            half, half, half,
            pltpu.SemaphoreType.DMA((3, G)),
            pltpu.SemaphoreType.DMA,
            pltpu.SemaphoreType.DMA((10,)),
            pltpu.SemaphoreType.DMA((10,)),
            many, many, many, many, many, many, many, many,
        ],
        compiler_params=pltpu.CompilerParams(
            collective_id=0, has_side_effects=True, vmem_limit_bytes=VLIM * 1024 * 1024
        ),
    )(density, momentum, energy, increment)
    return pl.pallas_call(
        last_kernel,
        out_shape=(
            jax.ShapeDtypeStruct((5, X, Y, L), f32),
            jax.ShapeDtypeStruct((5, X, Y, L), f32),
        ),
        in_specs=[vmem] * 3,
        out_specs=(hbm, hbm),
        scratch_shapes=[
            pltpu.VMEM((5, X, Y, L), f32),
            pltpu.SemaphoreType.DMA((X // LAST_STEP + 1,)),
        ],
        compiler_params=pltpu.CompilerParams(vmem_limit_bytes=16 * 1024 * 1024),
    )(part, register, carry)


def solution(mesh):
    in_specs = (
        P("gx", "gy", "gz"),
        P(None, "gx", "gy", "gz"),
        P("gx", "gy", "gz"),
        P(None, "gx", "gy", "gz"),
    )
    out_specs = (P(None, "gx", "gy", "gz"), P(None, "gx", "gy", "gz"))
    return jax.shard_map(
        functools.partial(section, mesh.shape["gx"], mesh.shape["gz"]),
        mesh=mesh,
        in_specs=in_specs,
        out_specs=out_specs,
        check_vma=False,
    )
```
